512 devices in a mesh: tile: 128 (over z, y, core), gz: 4 (over x).
Axes of the slice: x: 4, y: 8, z: 8, core: 2. Of those that a mesh axis runs over, the one named last changes fastest.
Arguments:
- images: bfloat16 [32768, 3, 16, 128], P('tile', None, 'gz'), may hold values from 0.19921875 to 2
- partner: int32 [128], replicated, may hold values from 0 to 127, as said below
- dest: int32 [16384, 1], P('tile'), may hold values from 0 to 127; in each aligned block of 128 rows (0 to 127, 128 to 255, ...) at most 2 rows name the same one
- offset: int32 [16384], P('tile'), may hold values from 0 to 254
- extent: int32 [16384], P('tile'), may hold values from 1 to 2
Outputs:
- corrected: bfloat16 [32768, 3, 16, 128], P('tile', None, 'gz')
- joined: bfloat16 [32768, 3, 16, 128], P('tile', None, 'gz')
The draws below stay inside these ranges and needn't reach their ends.
Inputs may be any that keep to these rules, and one draw needn't show every extreme that they name: partner[partner[t]] = t; partner[t] is t (no neighbour) or differs from t in exactly one bit of the index. `dest`: in each aligned block of 128 rows (one tile's pieces) no group is named more than 2 times, a bound that some block reaches.
All inputs are finite; a program needn't handle non-finite values.
Results may differ from the reference program's by a relative error of at most 0.0024.
Values may be sent and summed in bfloat16 or wider, within the bound.
No kernel may reach another device: no remote copies, remote signals or barrier semaphores. Data moves between devices by JAX's collectives and lax.ppermute only.
A program may use at most 64 MiB of HBM per device.

```python
import math
import jax
import jax.numpy as jnp
import numpy as np
from jax import lax

CH = 3
OV = 128
PL = 2
CAP = 2
TILES = 128
PIECES = 128
Y = 256
FR = 256
Z = 16


def draw_partner(key, part):
    index = jnp.arange(TILES, dtype=jnp.int32)
    levels = TILES.bit_length() - 1
    order = jax.random.permutation(jax.random.fold_in(key, 7), levels).astype(jnp.int32)
    paired = index
    unpaired = jnp.ones((TILES,), dtype=bool)
    for turn in range(levels):
        flip_bit = jnp.left_shift(jnp.int32(1), order[turn])
        other = jnp.bitwise_xor(index, flip_bit)
        coin = jax.random.randint(jax.random.fold_in(key, 100 + turn), (TILES,), 0, 2)
        lowest = jnp.minimum(index, other)
        taken = unpaired & unpaired[other] & (coin[lowest] == 1)
        paired = jnp.where(taken, other, paired)
        unpaired = unpaired & jnp.logical_not(taken)
    return paired.astype(jnp.int32)


def with_ends(entries, rng, least, top_value):
    shape = entries.shape
    place = [jax.random.randint(jax.random.fold_in(rng, axis), (), 0, shape[axis]) for axis in range(len(shape))]
    entries = entries.at[tuple(place)].set(least)
    longest = shape.index(max(shape))
    place[longest] = (place[longest] + 1) % shape[longest]
    return entries.at[tuple(place)].set(top_value)


def level_of(rng, shape, split, least, top_value):
    level = 1.0
    for axis_at, parts in split:
        heights = jax.random.uniform(jax.random.fold_in(jax.random.fold_in(rng, 6), axis_at), (parts,), jnp.float32, least / len(split), top_value / len(split))
        level = level * jnp.repeat(jnp.exp(heights), shape[axis_at] // parts).reshape((-1,) + (1,) * (len(shape) - 1 - axis_at))
    return level


def deal_out(own_key, own, number, rows, count, top, most, slope):
    ranking = jax.random.permutation(own_key, count)
    heavy_load, usual = shares(count, rows * top, most, slope, True), shares(count, rows * top, most, slope, False)
    places = jnp.arange(count)

    def named(lengths, offset_by):
        used = int((lengths > 0).sum())
        fixed = max(1, used // 4)
        passed = fixed + (places - fixed + offset_by * (used - fixed)) % max(1, count - fixed)
        return jnp.zeros((count,), jnp.int32).at[ranking[jnp.where(places < fixed, places, passed)]].set(jnp.asarray(lengths, jnp.int32))

    lengths = jnp.where(number % 4 == 0, named(heavy_load, number // 4), named(usual, number - number // 4 - 1))
    mixed = jax.random.permutation(jax.random.fold_in(own, 3), count)
    donor, taker = mixed[0:count // 2 * 2:2], mixed[1:count // 2 * 2:2]
    margin = jnp.minimum(lengths[donor] - 1, most - lengths[taker]) // 2
    margin = jnp.where((donor == ranking[0]) | (taker == ranking[0]) | (lengths[taker] == 0), 0, jnp.maximum(margin, 0))
    passed = jax.random.randint(jax.random.fold_in(own, 4), (count // 2,), 0, 1 << 20) % (margin + 1)
    lengths = lengths.at[donor].add(-passed).at[taker].add(passed)
    members = jnp.searchsorted(jnp.cumsum(lengths), jnp.arange(rows * top), side="right").astype(jnp.int32)
    grid = members.reshape(top, rows).T
    grid = grid[jax.random.permutation(jax.random.fold_in(own, 1), rows)]
    offset_by = jax.random.randint(jax.random.fold_in(own, 2), (rows, 1), 0, top)
    return jnp.take_along_axis(grid, (jnp.arange(top)[None, :] + offset_by) % top, axis=1)


def shares(number_of, total, most, skew, full):
    weights = [(1 << 20) // math.isqrt(grade ** skew) + 1 for grade in range(1, number_of + 1)]
    largest = most if full else min(most, max(-(-total // number_of), total * weights[0] // sum(weights)))
    least = 1 if total - largest >= number_of - 1 else 0
    given, rest = [largest] + [least] * (number_of - 1), total - largest - least * (number_of - 1)
    while rest > 0:
        free = [i for i in range(1, number_of) if given[i] < largest] or [i for i in range(1, number_of) if given[i] < most]
        whole, remaining = sum([weights[i] for i in free]), rest
        for i in free:
            addition = min(most - given[i], max(1, remaining * weights[i] // whole), rest)
            given[i] = given[i] + addition
            rest = rest - addition
    return np.array(given)


def setup_inputs(seed: int = 0) -> dict:
    seeds = jax.random.split(jax.random.key(seed), 6)
    images = jnp.clip(0.19921875 + 1.8007812 * jax.random.uniform(seeds[0], (TILES * Y, CH, Z, OV), jnp.float32) ** level_of(seeds[0], (TILES * Y, CH, Z, OV), ((0, 128), (2, 4)), -0.2, 0.2), 0.19921875, 2.0).astype(jnp.bfloat16)
    partner = draw_partner(jax.random.fold_in(seeds[5], 71), 0)
    dest_keys = jax.random.split(jax.random.fold_in(seeds[2], 1), (TILES * PIECES) // PIECES)
    dest_turns = jax.random.permutation(jax.random.fold_in(seeds[2], 3), (TILES * PIECES) // PIECES)
    dest = jax.vmap(lambda own, number: deal_out(jax.random.fold_in(seeds[2], 2), own, number, PIECES, TILES, 1, CAP, 2))(dest_keys, dest_turns).reshape((TILES * PIECES, 1))
    offset = with_ends(jax.random.randint(seeds[3], (TILES * PIECES,), 0, FR - PL + 1), jax.random.fold_in(seeds[3], 1), 0, FR - PL).astype(jnp.int32)
    extent = with_ends(jax.random.randint(seeds[4], (TILES * PIECES,), 1, PL + 1), jax.random.fold_in(seeds[4], 1), 1, PL).astype(jnp.int32)
    return dict(images=images, partner=partner, dest=dest, offset=offset, extent=extent)


gauss_raw = [math.exp(-0.5 * k * k) for k in range(-2, 3)]
gauss_taps = [w / sum(gauss_raw) for w in gauss_raw]


def central(values, axis):
    size = values.shape[axis]
    padded = jnp.pad(values, [(1, 1) if a == axis else (0, 0) for a in range(values.ndim)])
    upper = lax.slice_in_dim(padded, 2, size + 2, axis=axis)
    lower = lax.slice_in_dim(padded, 0, size, axis=axis)
    return (upper - lower) * 0.5


def smooth(values, axis):
    size = values.shape[axis]
    reach = len(gauss_taps) // 2
    padded = jnp.pad(values, [(reach, reach) if a == axis else (0, 0) for a in range(values.ndim)])
    total = jnp.zeros(values.shape, jnp.float32)
    for k in range(len(gauss_taps)):
        total = total + gauss_taps[k] * lax.slice_in_dim(padded, k, k + size, axis=axis)
    return total


def correct_channel(own, facing):
    first = own.astype(jnp.float32)
    second = facing.astype(jnp.float32)
    dy_a, dz_a, dx_a = central(first, 0), central(first, 1), central(first, 2)
    dy_b, dz_b, dx_b = central(second, 0), central(second, 1), central(second, 2)
    prod_one = first * second + dy_a * dy_b + dz_a * dz_b + dx_a * dx_b
    prod_two = second * second + dy_b * dy_b + dz_b * dz_b + dx_b * dx_b
    smooth_one = smooth(smooth(smooth(prod_one, 1), 0), 2)
    smooth_two = smooth(smooth(smooth(prod_two, 1), 0), 2)
    return (first * (smooth_one + 1.0) / (smooth_two + 1.0)).astype(jnp.bfloat16)


def reference(images, partner, dest, offset, extent):
    tiles = images.reshape(TILES, Y, CH, Z, OV)

    def one_tile(index):
        own = tiles[index]
        other = partner[index]
        facing = jnp.flip(tiles[other], axis=3)
        facing = jnp.where(other == index, jnp.zeros_like(facing), facing)
        outs = [correct_channel(own[:, c], facing[:, c]) for c in range(CH)]
        return jnp.stack(outs, axis=1)

    corrected = lax.map(one_tile, jnp.arange(TILES, dtype=jnp.int32))
    corrected = corrected.reshape(TILES * Y, CH, Z, OV)
    rows = jnp.arange(TILES * Y, dtype=jnp.int32)
    piece = rows // PL
    within = rows % PL
    target = dest[:, 0][piece] * FR + offset[piece] + within
    live = (within < extent[piece]).astype(jnp.float32)
    counts = jax.ops.segment_sum(live, target, num_segments=TILES * FR)
    outs = []
    for c in range(CH):
        values = corrected[:, c].reshape(TILES * Y, Z * OV).astype(jnp.float32) * live[:, None]
        sums = jax.ops.segment_sum(values, target, num_segments=TILES * FR)
        joined_c = (sums / jnp.maximum(counts, 1.0)[:, None]).astype(jnp.bfloat16)
        outs.append(joined_c.reshape(TILES * FR, Z, OV))
    joined = jnp.stack(outs, axis=1)
    return corrected, joined
```

```python
import math

import jax
import jax.numpy as jnp
from jax import lax
from jax.experimental import pallas as pl
from jax.experimental.pallas import tpu as pltpu
from jax.sharding import PartitionSpec as P

CAP = 2
HALO = 3

gauss_raw = [math.exp(-0.5 * k * k) for k in range(-2, 3)]
gauss_taps = [w / sum(gauss_raw) for w in gauss_raw]

F32 = jnp.float32
BF16 = jnp.bfloat16


def dot(a, b):
    return jnp.dot(a, b, preferred_element_type=F32)


def iotas(rows, cols):
    return (
        lax.broadcasted_iota(jnp.int32, (rows, cols), 0),
        lax.broadcasted_iota(jnp.int32, (rows, cols), 1),
    )


def band(i, j):
    total = jnp.zeros(i.shape, F32)
    for k in range(5):
        total = jnp.where(i - j == k - 2, jnp.float32(gauss_taps[k]), total)
    high = total.astype(BF16)
    return high, (total - high.astype(F32)).astype(BF16)


def split(v):
    high = v.astype(BF16)
    return high, (v - high.astype(F32)).astype(BF16)


def correct_kernel(
    flags, own, own_lo, own_hi, fac, fac_lo, fac_hi, out, b, dxa, dxb, dya, dyb, deep
):
    rows, cols = own.shape[2:]
    depth = own.shape[1]
    wide = depth + 2 * HALO
    low, high, face = flags[0], flags[1], flags[2]

    def plane(mid, lo, hi, k):
        if k < HALO:
            return lo, k
        if k < HALO + depth:
            return mid, k - HALO
        return hi, k - HALO - depth

    i, j = iotas(cols, cols)
    half = jnp.float32(0.5)
    zero = jnp.float32(0.0)
    turn = jnp.where(i + j == cols - 1, face, zero)
    turned_dx = jnp.where(i + j == cols - 2, half * face, zero) - jnp.where(
        i + j == cols, half * face, zero
    )
    turn = jnp.concatenate([turn, turned_dx], axis=1).astype(BF16)
    across = (jnp.where(i == j + 1, half, zero) - jnp.where(i == j - 1, half, zero)).astype(BF16)
    g_hi, g_lo = band(i, j)
    smooth_x = jnp.concatenate(
        [
            jnp.concatenate([g_hi, g_lo], axis=1),
            jnp.concatenate([g_hi, jnp.zeros_like(g_lo)], axis=1),
        ],
        axis=0,
    )
    i, j = iotas(rows, rows)
    along = (jnp.where(j == i + 1, half, zero) - jnp.where(j == i - 1, half, zero)).astype(BF16)
    y_hi, y_lo = band(i, j)
    smooth_y = jnp.concatenate([y_hi, y_lo], axis=0)

    for k in range(wide):
        ref, at = plane(fac, fac_lo, fac_hi, k)
        both = dot(ref[0, at], turn)
        b[k] = both[:, :cols]
        if 0 < k < wide - 1:
            dxb[k - 1] = both[:, cols:]
            ref, at = plane(own, own_lo, own_hi, k)
            a = ref[0, at]
            dxa[k - 1] = dot(a, across)
            dy = dot(along, jnp.concatenate([a, both[:, :cols].astype(BF16)], axis=1))
            dya[k - 1] = dy[:, :cols]
            dyb[k - 1] = dy[:, cols:]

    step = 32

    def chunk(r, carry):
        at_rows = pl.ds(pl.multiple_of(r * step, step), step)

        def a_of(k):
            ref, at = plane(own, own_lo, own_hi, k)
            return ref[0, at, at_rows, :].astype(F32)

        one = [jnp.zeros((step, cols), F32) for _ in range(depth)]
        two = [jnp.zeros((step, cols), F32) for _ in range(depth)]
        for k in range(1, wide - 1):
            av, bv = a_of(k), b[k, at_rows, :]
            dza = (a_of(k + 1) - a_of(k - 1)) * half
            dzb = (b[k + 1, at_rows, :] - b[k - 1, at_rows, :]) * half
            ya, yb = dya[k - 1, at_rows, :], dyb[k - 1, at_rows, :]
            xa, xb = dxa[k - 1, at_rows, :], dxb[k - 1, at_rows, :]
            p1 = av * bv + ya * yb + dza * dzb + xa * xb
            p2 = bv * bv + yb * yb + dzb * dzb + xb * xb
            if k < HALO:
                p1, p2 = p1 * low, p2 * low
            if k >= HALO + depth:
                p1, p2 = p1 * high, p2 * high
            for z in range(depth):
                tap = k - (HALO + z) + 2
                if 0 <= tap < 5:
                    one[z] = one[z] + gauss_taps[tap] * p1
                    two[z] = two[z] + gauss_taps[tap] * p2
        for z in range(depth):
            for s, v in ((0, one[z]), (1, two[z])):
                h, l = split(v)
                deep[2 * z + s, at_rows, :cols] = h
                deep[2 * z + s, at_rows, cols:] = l
        return carry

    lax.fori_loop(0, rows // step, chunk, 0)

    for z in range(depth):
        parts = []
        for s in range(2):
            r = dot(deep[2 * z + s], smooth_x)
            parts.append(split(r[:, :cols] + r[:, cols:]))
        r_hi = jnp.concatenate([parts[0][0], parts[1][0]], axis=1)
        r_lo = jnp.concatenate([parts[0][1], parts[1][1]], axis=1)
        main = dot(smooth_y, r_hi)
        q = main[:rows] + main[rows:] + dot(y_hi, r_lo)
        a = own[0, z].astype(F32)
        out[0, z] = (a * (q[:, :cols] + 1.0) / (q[:, cols:] + 1.0)).astype(BF16)


def correct(flags, own, own_lo, own_hi, fac, fac_lo, fac_hi):
    chans, depth, rows, cols = own.shape
    wide = depth + 2 * HALO

    def spec(n):
        return pl.BlockSpec((1, n, rows, cols), lambda c: (c, 0, 0, 0))

    def vmem(n):
        return pltpu.VMEM((n, rows, cols), F32)

    return pl.pallas_call(
        correct_kernel,
        grid=(chans,),
        in_specs=[pl.BlockSpec(memory_space=pltpu.SMEM)]
        + [spec(depth), spec(HALO), spec(HALO)] * 2,
        out_specs=spec(depth),
        out_shape=jax.ShapeDtypeStruct(own.shape, BF16),
        scratch_shapes=[
            vmem(wide),
            vmem(wide - 2),
            vmem(wide - 2),
            vmem(wide - 2),
            vmem(wide - 2),
            pltpu.VMEM((2 * depth, rows, 2 * cols), BF16),
        ],
        compiler_params=pltpu.CompilerParams(vmem_limit_bytes=24 << 20),
        name="correct",
    )(flags, own, own_lo, own_hi, fac, fac_lo, fac_hi)


def pack_kernel(code, planes, out):
    count, rows, cols = planes.shape
    step = 256
    for m in range(out.shape[0] // step):
        i = lax.broadcasted_iota(jnp.int32, (step, 2 * rows), 0) + m * step
        pick = jnp.where(i == code[...], jnp.float32(1.0), jnp.float32(0.0)).astype(BF16)
        for n in range(count // 4):
            left = planes[4 * n : 4 * n + 2].reshape(2 * rows, cols)
            right = planes[4 * n + 2 : 4 * n + 4].reshape(2 * rows, cols)
            v = dot(pick, jnp.concatenate([left, right], axis=1))
            out[m * step : (m + 1) * step, 2 * n * cols : 2 * (n + 1) * cols] = v.astype(BF16)


def pack(code, planes, blocks):
    count, rows, cols = planes.shape
    return pl.pallas_call(
        pack_kernel,
        out_shape=jax.ShapeDtypeStruct((blocks * 8, count // 2 * cols), BF16),
        compiler_params=pltpu.CompilerParams(vmem_limit_bytes=16 << 20),
        name="pack",
    )(code, planes)


def join_kernel(code, got, out):
    count, rows, cols = out.shape
    lines = got.shape[0]
    i = lax.broadcasted_iota(jnp.int32, (rows, lines), 0)
    one, zero = jnp.float32(1.0), jnp.float32(0.0)
    counts = None
    for h in range(2):
        place = jnp.where(i == code[h : h + 1, :], one, zero).astype(BF16)
        if h == 0:
            counts = dot(place, jnp.ones((lines, cols), BF16))
            counts = jnp.maximum(counts, 1.0)
        for n in range(count // 4):
            v = dot(place, got[:, 2 * n * cols : 2 * (n + 1) * cols])
            out[4 * n + h] = (v[:, :cols] / counts).astype(BF16)
            out[4 * n + 2 + h] = (v[:, cols:] / counts).astype(BF16)


def join(code, got, rows, cols):
    count = got.shape[1] // cols * 2
    return pl.pallas_call(
        join_kernel,
        out_shape=jax.ShapeDtypeStruct((count, rows, cols), BF16),
        compiler_params=pltpu.CompilerParams(vmem_limit_bytes=16 << 20),
        name="join",
    )(code, got)


def halo(block):
    count = lax.axis_size("gz")
    forward = [(i, i + 1) for i in range(count - 1)]
    backward = [(i + 1, i) for i in range(count - 1)]
    depth = block.shape[1]
    low = lax.ppermute(block[:, depth - HALO :], "gz", forward)
    high = lax.ppermute(block[:, :HALO], "gz", backward)
    return low, high


def swap(blocks):
    return lax.all_to_all(blocks, "tile", split_axis=0, concat_axis=0, tiled=True)


def body(images, partner, dest, offset, extent):
    ntile = lax.axis_size("tile")
    tile = lax.axis_index("tile")
    plane_idx = lax.axis_index("gz")
    nplane = lax.axis_size("gz")
    rows, chans, depth, cols = images.shape
    lines = chans * depth * rows
    own = jnp.transpose(images, (1, 2, 0, 3))
    own = lax.optimization_barrier(own)
    own_lo, own_hi = halo(own)
    spread = swap(own.reshape(ntile, lines // ntile, cols))
    picked = jnp.take(spread, partner, axis=0, mode="clip")
    fac = swap(picked).reshape(chans, depth, rows, cols)

    targets = dest[:, 0]
    order_idx = jnp.arange(ntile, dtype=jnp.int32)
    same_owner = targets[:, None] == targets[None, :]
    earlier = order_idx[:, None] > order_idx[None, :]
    slot = jnp.sum((same_owner & earlier).astype(jnp.int32), axis=1)
    slots = jnp.arange(CAP, dtype=jnp.int32)
    select = (order_idx[:, None, None] == targets[None, None, :]) & (
        slots[None, :, None] == slot[None, None, :]
    )
    label = offset * 4 + extent
    labels = jnp.sum(jnp.where(select, label[None, None, :], 0), axis=2)
    within = jnp.arange(2, dtype=jnp.int32)
    code = (targets * 8 + slot * 2)[:, None] + within[None, :]
    code = code.reshape(1, rows)
    code = jnp.concatenate([code, code + 4], axis=1)

    fac, labels = lax.optimization_barrier((fac, labels))
    fac_lo, fac_hi = halo(fac)
    info = swap(labels)

    flags = jnp.stack(
        [plane_idx > 0, plane_idx < nplane - 1, partner[tile] != tile]
    ).astype(F32)
    corrected = correct(flags, own, own_lo, own_hi, fac, fac_lo, fac_hi)
    planes = corrected.reshape(chans * depth, rows, cols)
    outgoing = pack(code, planes, ntile)
    received = swap(outgoing.reshape(ntile, 8, outgoing.shape[1]))

    start, span = info // 4, info % 4
    spots = jnp.where(within < span[:, :, None], start[:, :, None] + within, -1)
    spots = spots.reshape(ntile, 2 * CAP)
    none = jnp.full_like(spots, -1)
    code_in = jnp.stack(
        [
            jnp.concatenate([spots, none], axis=1).reshape(-1),
            jnp.concatenate([none, spots], axis=1).reshape(-1),
        ]
    )
    joined = join(code_in, received.reshape(ntile * 8, -1), rows, cols)

    def home(v):
        return jnp.transpose(v.reshape(chans, depth, rows, cols), (2, 0, 1, 3))

    return home(corrected), home(joined)


def solution(mesh):
    in_specs = (P("tile", None, "gz", None), P(), P("tile", None), P("tile"), P("tile"))
    out_specs = (P("tile", None, "gz", None), P("tile", None, "gz", None))
    return jax.shard_map(body, mesh=mesh, in_specs=in_specs, out_specs=out_specs, check_vma=False)
```

```python
import functools
import math

import jax
import jax.numpy as jnp
from jax import lax
from jax.experimental import pallas as pl
from jax.experimental.pallas import tpu as pltpu
from jax.sharding import PartitionSpec as P

CAP = 2
HALO = 3

gauss_raw = [math.exp(-0.5 * k * k) for k in range(-2, 3)]
gauss_taps = [w / sum(gauss_raw) for w in gauss_raw]

F32 = jnp.float32
BF16 = jnp.bfloat16


def dot(a, b):
    return jnp.dot(a, b, preferred_element_type=F32)


def iotas(rows, cols):
    return (
        lax.broadcasted_iota(jnp.int32, (rows, cols), 0),
        lax.broadcasted_iota(jnp.int32, (rows, cols), 1),
    )


def band(i, j):
    total = jnp.zeros(i.shape, F32)
    for k in range(5):
        total = jnp.where(i - j == k - 2, jnp.float32(gauss_taps[k]), total)
    high = total.astype(BF16)
    return high, (total - high.astype(F32)).astype(BF16)


def split(v):
    high = v.astype(BF16)
    return high, (v - high.astype(F32)).astype(BF16)


def matrices(rows, cols, face):
    i, j = iotas(cols, cols)
    half = jnp.float32(0.5)
    zero = jnp.float32(0.0)
    turn = jnp.where(i + j == cols - 1, face, zero)
    turned_dx = jnp.where(i + j == cols - 2, half * face, zero) - jnp.where(
        i + j == cols, half * face, zero
    )
    turn = jnp.concatenate([turn, turned_dx], axis=1).astype(BF16)
    across = (jnp.where(i == j + 1, half, zero) - jnp.where(i == j - 1, half, zero)).astype(BF16)
    g_hi, g_lo = band(i, j)
    smooth_x = jnp.concatenate(
        [
            jnp.concatenate([g_hi, g_lo], axis=1),
            jnp.concatenate([g_hi, jnp.zeros_like(g_lo)], axis=1),
        ],
        axis=0,
    )
    i, j = iotas(rows, rows)
    along = (jnp.where(j == i + 1, half, zero) - jnp.where(j == i - 1, half, zero)).astype(BF16)
    smooth_y = jnp.concatenate(band(i, j), axis=0)
    return turn, across, along, smooth_x, smooth_y


def prepare_kernel(across, along, own, own_lo, own_hi, a10, dxa, dya):
    depth, _, rows, cols = own.shape
    for k in range(depth + 2 * HALO):
        if k < HALO:
            a = own_lo[k, 0]
        elif k < HALO + depth:
            a = own[k - HALO, 0]
        else:
            a = own_hi[k - HALO - depth, 0]
        a10[0, k] = a
        if 0 < k < depth + 2 * HALO - 1:
            dxa[0, k - 1] = dot(a, across[...])
            if k % 2 == 0:
                dy = dot(along[...], jnp.concatenate([before, a], axis=1))
                dya[0, k - 2] = dy[:, :cols]
                dya[0, k - 1] = dy[:, cols:]
        before = a


def prepare(across, along, own, own_lo, own_hi):
    depth, chans, rows, cols = own.shape
    wide = depth + 2 * HALO

    def spec(n):
        return pl.BlockSpec((n, 1, rows, cols), lambda c: (0, c, 0, 0))

    def result(n):
        return pl.BlockSpec((1, n, rows, cols), lambda c: (c, 0, 0, 0))

    def whole(m):
        return pl.BlockSpec(m.shape, lambda c: (0, 0))

    def shape(n, dtype):
        return jax.ShapeDtypeStruct((chans, n, rows, cols), dtype)

    return pl.pallas_call(
        prepare_kernel,
        grid=(chans,),
        in_specs=[whole(across), whole(along), spec(depth), spec(HALO), spec(HALO)],
        out_specs=[result(wide), result(wide - 2), result(wide - 2)],
        out_shape=[shape(wide, BF16), shape(wide - 2, F32), shape(wide - 2, F32)],
        compiler_params=pltpu.CompilerParams(vmem_limit_bytes=10 << 20),
        name="prepare",
    )(across, along, own, own_lo, own_hi)


def correct_kernel(
    chan,
    flags,
    turn,
    along,
    smooth_x,
    smooth_y,
    a10_far,
    dxa_far,
    dya_far,
    fac,
    fac_lo,
    fac_hi,
    out,
    b,
    dxb,
    dyb,
    deep,
    a10,
    dxa,
    dya,
    sems,
):
    depth, _, rows, cols = fac.shape
    wide = depth + 2 * HALO
    fetches = [
        pltpu.make_async_copy(far.at[chan], near, sems.at[n])
        for n, (far, near) in enumerate(((a10_far, a10), (dxa_far, dxa), (dya_far, dya)))
    ]
    for fetch in fetches:
        fetch.start()
    low, high = flags[0], flags[1]
    half = jnp.float32(0.5)
    for k in range(wide):
        if k < HALO:
            f = fac_lo[k]
        elif k < HALO + depth:
            f = fac[k - HALO, chan]
        else:
            f = fac_hi[k - HALO - depth]
        both = dot(f, turn[...])
        b[k] = both[:, :cols]
        now = both[:, :cols].astype(BF16)
        if 0 < k < wide - 1:
            dxb[k - 1] = both[:, cols:]
            if k % 2 == 0:
                dy = dot(along[...], jnp.concatenate([before, now], axis=1))
                dyb[k - 2] = dy[:, :cols]
                dyb[k - 1] = dy[:, cols:]
        before = now
    for fetch in fetches:
        fetch.wait()

    step = 32

    def chunk(r, carry):
        at_rows = pl.ds(pl.multiple_of(r * step, step), step)

        def a_of(k):
            return a10[k, at_rows, :].astype(F32)

        one = [jnp.zeros((step, cols), F32) for _ in range(depth)]
        two = [jnp.zeros((step, cols), F32) for _ in range(depth)]
        for k in range(1, wide - 1):
            av, bv = a_of(k), b[k, at_rows, :]
            dza = (a_of(k + 1) - a_of(k - 1)) * half
            dzb = (b[k + 1, at_rows, :] - b[k - 1, at_rows, :]) * half
            ya, yb = dya[k - 1, at_rows, :], dyb[k - 1, at_rows, :]
            xa, xb = dxa[k - 1, at_rows, :], dxb[k - 1, at_rows, :]
            p1 = av * bv + ya * yb + dza * dzb + xa * xb
            p2 = bv * bv + yb * yb + dzb * dzb + xb * xb
            if k < HALO:
                p1, p2 = p1 * low, p2 * low
            if k >= HALO + depth:
                p1, p2 = p1 * high, p2 * high
            for z in range(depth):
                tap = k - (HALO + z) + 2
                if 0 <= tap < 5:
                    one[z] = one[z] + gauss_taps[tap] * p1
                    two[z] = two[z] + gauss_taps[tap] * p2
        for z in range(depth):
            for s, v in ((0, one[z]), (1, two[z])):
                h, l = split(v)
                deep[2 * z + s, at_rows, :cols] = h
                deep[2 * z + s, at_rows, cols:] = l
        return carry

    lax.fori_loop(0, rows // step, chunk, 0)

    for z in range(depth):
        parts = []
        for s in range(2):
            r = dot(deep[2 * z + s], smooth_x[...])
            parts.append(split(r[:, :cols] + r[:, cols:]))
        r_hi = jnp.concatenate([parts[0][0], parts[1][0]], axis=1)
        r_lo = jnp.concatenate([parts[0][1], parts[1][1]], axis=1)
        main = dot(smooth_y[...], r_hi)
        q = main[:rows] + main[rows:] + dot(smooth_y[:rows], r_lo)
        a = a10[z + HALO].astype(F32)
        out[z] = (a * (q[:, :cols] + 1.0) / (q[:, cols:] + 1.0)).astype(BF16)


def correct(chan, flags, turn, along, smooth_x, smooth_y, a10, dxa, dya, fac, fac_lo, fac_hi):
    depth, _, rows, cols = fac.shape
    wide = depth + 2 * HALO

    def vmem(n):
        return pltpu.VMEM((n, rows, cols), F32)

    near = pl.BlockSpec(memory_space=pltpu.VMEM)
    far = pl.BlockSpec(memory_space=pltpu.HBM)
    return pl.pallas_call(
        functools.partial(correct_kernel, chan),
        in_specs=[pl.BlockSpec(memory_space=pltpu.SMEM)] + [near] * 4 + [far] * 3 + [near] * 3,
        out_specs=near,
        out_shape=jax.ShapeDtypeStruct((depth, rows, cols), BF16),
        scratch_shapes=[
            vmem(wide),
            vmem(wide - 2),
            vmem(wide - 2),
            pltpu.VMEM((2 * depth, rows, 2 * cols), BF16),
            pltpu.VMEM((wide, rows, cols), BF16),
            vmem(wide - 2),
            vmem(wide - 2),
            pltpu.SemaphoreType.DMA((3,)),
        ],
        compiler_params=pltpu.CompilerParams(vmem_limit_bytes=12 << 20),
        cost_estimate=pl.CostEstimate(
            flops=2000000000, bytes_accessed=12000000, transcendentals=0
        ),
        name="correct",
    )(flags, turn, along, smooth_x, smooth_y, a10, dxa, dya, fac, fac_lo, fac_hi)


def pack_kernel(code, first, second, third, out, held, sems):
    rows, cols = first.shape[1:]
    step = held.shape[0] // sems.shape[0]
    copies = []
    for m in range(sems.shape[0]):
        at = pl.ds(m * step, step)
        i = lax.broadcasted_iota(jnp.int32, (step, 2 * rows), 0) + m * step
        pick = jnp.where(i == code[...], jnp.float32(1.0), jnp.float32(0.0)).astype(BF16)
        for n, planes in enumerate((first, second, third)):
            left = planes[0:2].reshape(2 * rows, cols)
            right = planes[2:4].reshape(2 * rows, cols)
            v = dot(pick, jnp.concatenate([left, right], axis=1))
            held[m * step : (m + 1) * step, 2 * n * cols : 2 * (n + 1) * cols] = v.astype(BF16)
        copies.append(pltpu.make_async_copy(held.at[at], out.at[at], sems.at[m]))
        copies[-1].start()
    for copy in copies:
        copy.wait()


def pack(code, planes, blocks):
    depth, rows, cols = planes[0].shape
    shape = (blocks * 8, len(planes) * depth // 2 * cols)
    return pl.pallas_call(
        pack_kernel,
        in_specs=[pl.BlockSpec(memory_space=pltpu.VMEM)] * (1 + len(planes)),
        out_specs=pl.BlockSpec(memory_space=pltpu.HBM),
        out_shape=jax.ShapeDtypeStruct(shape, BF16),
        scratch_shapes=[pltpu.VMEM(shape, BF16), pltpu.SemaphoreType.DMA((4,))],
        compiler_params=pltpu.CompilerParams(vmem_limit_bytes=6 << 20),
        name="pack",
    )(code, *planes)


def join_kernel(code, got, out):
    count, rows, cols = out.shape
    lines = got.shape[0]
    i = lax.broadcasted_iota(jnp.int32, (rows, lines), 0)
    one, zero = jnp.float32(1.0), jnp.float32(0.0)
    counts = None
    for h in range(2):
        place = jnp.where(i == code[h : h + 1, :], one, zero).astype(BF16)
        if h == 0:
            counts = dot(place, jnp.ones((lines, cols), BF16))
            counts = jnp.maximum(counts, 1.0)
        for n in range(count // 4):
            v = dot(place, got[:, 2 * n * cols : 2 * (n + 1) * cols])
            out[4 * n + h] = (v[:, :cols] / counts).astype(BF16)
            out[4 * n + 2 + h] = (v[:, cols:] / counts).astype(BF16)


def join(code, got, rows, cols):
    count = got.shape[1] // cols * 2
    return pl.pallas_call(
        join_kernel,
        out_shape=jax.ShapeDtypeStruct((count, rows, cols), BF16),
        compiler_params=pltpu.CompilerParams(vmem_limit_bytes=6 << 20),
        name="join",
    )(code, got)


def halo(block, axis):
    count = lax.axis_size("gz")
    forward = [(i, i + 1) for i in range(count - 1)]
    backward = [(i + 1, i) for i in range(count - 1)]
    depth = block.shape[axis]
    low = lax.ppermute(lax.slice_in_dim(block, depth - HALO, depth, axis=axis), "gz", forward)
    high = lax.ppermute(lax.slice_in_dim(block, 0, HALO, axis=axis), "gz", backward)
    return low, high


def gather_all(v, first, last):
    count = lax.axis_size("tile")
    for bit in range(first, last):
        other = lax.ppermute(v, "tile", [(i, i ^ (1 << bit)) for i in range(count)])
        v = jnp.concatenate([v, other], axis=0)
    return v


def swap(blocks):
    return lax.all_to_all(blocks, "tile", split_axis=0, concat_axis=0, tiled=True)


def body(images, partner, dest, offset, extent):
    ntile = lax.axis_size("tile")
    tile = lax.axis_index("tile")
    plane_idx = lax.axis_index("gz")
    nplane = lax.axis_size("gz")
    rows, chans, depth, cols = images.shape
    lines = chans * depth * rows
    own = jnp.transpose(images, (2, 1, 0, 3))
    own = lax.optimization_barrier(own)
    turn, across, along, smooth_x, smooth_y = matrices(
        rows, cols, (partner[tile] != tile).astype(F32)
    )
    targets = dest[:, 0]
    order_idx = jnp.arange(ntile, dtype=jnp.int32)
    label = (targets * 1024 + offset * 4 + extent)[None, :]
    early = 3
    spread = swap(own.reshape(ntile, lines // ntile, cols))
    label = gather_all(label, 0, early)
    partner, label = lax.optimization_barrier((partner, label))
    picked = jnp.take(spread, partner, axis=0, mode="clip")
    fac = swap(picked).reshape(depth, chans, rows, cols)
    own_lo, own_hi = halo(own, 0)
    a10, dxa, dya = prepare(across, along, own, own_lo, own_hi)
    label = gather_all(label, early, ntile.bit_length() - 1)

    same_owner = targets[:, None] == targets[None, :]
    earlier = order_idx[:, None] > order_idx[None, :]
    slot = jnp.sum((same_owner & earlier).astype(jnp.int32), axis=1)
    within = jnp.arange(2, dtype=jnp.int32)
    code = (targets * 8 + slot * 2)[:, None] + within[None, :]
    code = code.reshape(1, rows)
    code = jnp.concatenate([code, code + 4], axis=1)

    mine = (label // 1024) == tile
    spot = label % 1024
    head = jnp.min(jnp.where(mine, order_idx[None, :], ntile), axis=1, keepdims=True)
    is_head = order_idx[None, :] == head
    first = jnp.sum(jnp.where(mine & is_head, spot, 0), axis=1)
    second = jnp.sum(jnp.where(mine & ~is_head, spot, 0), axis=1)
    info = jnp.take(jnp.stack([first, second], axis=1), order_idx ^ tile, axis=0, mode="clip")
    start, span = info // 4, info % 4
    spots = jnp.where(within < span[:, :, None], start[:, :, None] + within, -1)
    spots = spots.reshape(ntile, 2 * CAP)
    none = jnp.full_like(spots, -1)
    code_in = jnp.stack(
        [
            jnp.concatenate([spots, none], axis=1).reshape(-1),
            jnp.concatenate([none, spots], axis=1).reshape(-1),
        ]
    )
    flags = jnp.stack([plane_idx > 0, plane_idx < nplane - 1]).astype(F32)
    fac, a10, dxa, dya, turn, code, code_in, flags = lax.optimization_barrier(
        (fac, a10, dxa, dya, turn, code, code_in, flags)
    )

    sides = [halo(fac[:, c], 0) for c in range(chans)]
    planes = [
        correct(c, flags, turn, along, smooth_x, smooth_y, a10, dxa, dya, fac, *sides[c])
        for c in range(chans)
    ]
    outgoing = pack(code, planes, ntile)
    received = swap(outgoing.reshape(ntile, 8, outgoing.shape[1]))
    joined = join(code_in, received.reshape(ntile * 8, -1), rows, cols)

    def home(v):
        return jnp.transpose(v.reshape(chans, depth, rows, cols), (2, 0, 1, 3))

    return home(jnp.stack(planes)), home(joined)


def solution(mesh):
    in_specs = (P("tile", None, "gz", None), P(), P("tile", None), P("tile"), P("tile"))
    out_specs = (P("tile", None, "gz", None), P("tile", None, "gz", None))
    return jax.shard_map(body, mesh=mesh, in_specs=in_specs, out_specs=out_specs, check_vma=False)
```

```python
import math

import jax
import jax.numpy as jnp
import numpy as np
from jax import lax
from jax.experimental import pallas as pl
from jax.experimental.pallas import tpu as pltpu
from jax.sharding import PartitionSpec as P

CAP = 2
HALO = 3

gauss_raw = [math.exp(-0.5 * k * k) for k in range(-2, 3)]
gauss_taps = [w / sum(gauss_raw) for w in gauss_raw]

F32 = jnp.float32
BF16 = jnp.bfloat16


def dot(a, b):
    return jnp.dot(a, b, preferred_element_type=F32)


def split(v):
    high = v.astype(BF16)
    return high, (v - high.astype(F32)).astype(BF16)


def constants(rows, cols):
    def near(n):
        i, j = np.indices((n, n))
        return i - j

    def band(n):
        total = np.zeros((n, n), np.float32)
        for k in range(5):
            total[near(n) == k - 2] = gauss_taps[k]
        high = total.astype(BF16)
        return high, (total - high.astype(np.float32)).astype(BF16)

    turn = np.eye(cols, dtype=np.float32)[:, ::-1].astype(BF16)
    gap = near(cols)
    across = (0.5 * (gap == 1) - 0.5 * (gap == -1)).astype(BF16)
    gap = near(rows)
    along = (0.5 * (gap == -1) - 0.5 * (gap == 1)).astype(BF16)
    high, low = (m[:, ::-1] for m in band(cols))
    smooth_x = np.block([[high, low], [high, np.zeros_like(low)]])
    smooth_y = np.concatenate(band(rows), axis=0)
    return turn, across, along, smooth_x, smooth_y


def plane_of(own, own_lo, own_hi, k):
    depth = own.shape[1]
    if k < HALO:
        return own_lo, k
    if k < HALO + depth:
        return own, k - HALO
    return own_hi, k - HALO - depth


def prepare_kernel(turn, across, along, own, own_lo, own_hi, a10, dxa, dya):
    depth, _, cols = own.shape[1:]
    for k in range(depth + 2 * HALO):
        ref, at = plane_of(own, own_lo, own_hi, k)
        a = dot(ref[0, at], turn[...]).astype(BF16)
        a10[0, k] = a
        if 0 < k < depth + 2 * HALO - 1:
            dxa[0, k - 1] = dot(a, across[...])
            if k % 2 == 0:
                dy = dot(along[...], jnp.concatenate([before, a], axis=1))
                dya[0, k - 2] = dy[:, :cols]
                dya[0, k - 1] = dy[:, cols:]
        before = a


def prepare(turn, across, along, own, own_lo, own_hi):
    chans, depth, rows, cols = own.shape
    wide = depth + 2 * HALO

    def spec(n):
        return pl.BlockSpec((1, n, rows, cols), lambda c: (c, 0, 0, 0))

    def whole(m):
        return pl.BlockSpec(m.shape, lambda c: (0, 0))

    def shape(n, dtype):
        return jax.ShapeDtypeStruct((chans, n, rows, cols), dtype)

    return pl.pallas_call(
        prepare_kernel,
        grid=(chans,),
        in_specs=[whole(turn), whole(across), whole(along)]
        + [spec(depth), spec(HALO), spec(HALO)],
        out_specs=[spec(wide), spec(wide - 2), spec(wide - 2)],
        out_shape=[shape(wide, BF16), shape(wide - 2, F32), shape(wide - 2, F32)],
        compiler_params=pltpu.CompilerParams(vmem_limit_bytes=60 << 20),
        name="prepare",
    )(turn, across, along, own, own_lo, own_hi)


def pack(code, planes, out, held, sems):
    chans, _, rows, cols = planes.shape
    step = held.shape[0] // sems.shape[0]
    copies = []
    for m in range(sems.shape[0]):
        at = pl.ds(m * step, step)
        i = lax.broadcasted_iota(jnp.int32, (step, 2 * rows), 0) + m * step
        pick = jnp.where(i == code[...], jnp.float32(1.0), jnp.float32(0.0)).astype(BF16)
        for n in range(chans):
            left = planes[n, 0:2].reshape(2 * rows, cols)
            right = planes[n, 2:4].reshape(2 * rows, cols)
            v = dot(pick, jnp.concatenate([left, right], axis=1))
            held[m * step : (m + 1) * step, 2 * n * cols : 2 * (n + 1) * cols] = v.astype(BF16)
        copies.append(pltpu.make_async_copy(held.at[at], out.at[at], sems.at[m]))
        copies[-1].start()
    for copy in copies:
        copy.wait()


def correct_kernel(
    flags,
    across,
    along,
    smooth_x,
    smooth_y,
    code,
    a10,
    dxa,
    dya,
    own,
    fac,
    fac_lo,
    fac_hi,
    out,
    sent,
    dxb,
    dyb,
    deep,
    kept,
    held,
    sems,
):
    chan = pl.program_id(0)
    depth, rows, cols = fac.shape[1:]
    wide = depth + 2 * HALO
    low, high = flags[0], flags[1]
    half = jnp.float32(0.5)
    for k in range(1, wide - 1):
        ref, at = plane_of(fac, fac_lo, fac_hi, k)
        now = ref[0, at]
        dxb[k - 1] = dot(now, across[...])
        if k % 2 == 0:
            dy = dot(along[...], jnp.concatenate([before, now], axis=1))
            dyb[k - 2] = dy[:, :cols]
            dyb[k - 1] = dy[:, cols:]
        before = now

    step = 32

    def chunk(r, carry):
        at_rows = pl.ds(pl.multiple_of(r * step, step), step)

        def a_of(k):
            return a10[0, k, at_rows, :].astype(F32)

        def b_of(k):
            ref, at = plane_of(fac, fac_lo, fac_hi, k)
            return ref[0, at, at_rows, :].astype(F32)

        one = [None] * depth
        two = [None] * depth
        a_last, av, a_next = None, a_of(0), a_of(1)
        b_last, bv, b_next = None, b_of(0), b_of(1)
        for k in range(1, wide - 1):
            a_last, av, a_next = av, a_next, a_of(k + 1)
            b_last, bv, b_next = bv, b_next, b_of(k + 1)
            dza = (a_next - a_last) * half
            dzb = (b_next - b_last) * half
            ya, yb = dya[0, k - 1, at_rows, :], dyb[k - 1, at_rows, :]
            xa, xb = dxa[0, k - 1, at_rows, :], dxb[k - 1, at_rows, :]
            p1 = av * bv + ya * yb + dza * dzb + xa * xb
            p2 = bv * bv + yb * yb + dzb * dzb + xb * xb
            if k < HALO:
                p1, p2 = p1 * low, p2 * low
            if k >= HALO + depth:
                p1, p2 = p1 * high, p2 * high
            for t in range(3):
                v1, v2 = gauss_taps[t] * p1, gauss_taps[t] * p2
                for z in {k - HALO + 2 - t, k - HALO - 2 + t}:
                    if 0 <= z < depth:
                        one[z] = v1 if one[z] is None else one[z] + v1
                        two[z] = v2 if two[z] is None else two[z] + v2
        for z in range(depth):
            for s, v in ((0, one[z]), (1, two[z])):
                h, l = split(v)
                deep[2 * z + s, at_rows, :cols] = h
                deep[2 * z + s, at_rows, cols:] = l
        return carry

    lax.fori_loop(0, rows // step, chunk, 0)

    for z in range(depth):
        parts = []
        for s in range(2):
            r = dot(deep[2 * z + s], smooth_x[...])
            parts.append(split(r[:, :cols] + r[:, cols:]))
        r_hi = jnp.concatenate([parts[0][0], parts[1][0]], axis=1)
        r_lo = jnp.concatenate([parts[0][1], parts[1][1]], axis=1)
        main = dot(smooth_y[...], r_hi)
        q = main[:rows] + main[rows:] + dot(smooth_y[:rows], r_lo)
        a = own[0, z].astype(F32)
        done = (a * (q[:, :cols] + 1.0) / (q[:, cols:] + 1.0)).astype(BF16)
        out[0, z] = done
        kept[chan, z] = done

    @pl.when(chan == kept.shape[0] - 1)
    def _():
        pack(code, kept, sent, held, sems)


def correct(
    flags, across, along, smooth_x, smooth_y, code, a10, dxa, dya, own, fac, fac_lo, fac_hi, blocks
):
    chans, depth, rows, cols = own.shape
    wide = depth + 2 * HALO
    packed = (blocks * 8, chans * depth // 2 * cols)

    def spec(n):
        return pl.BlockSpec((1, n, rows, cols), lambda c: (c, 0, 0, 0))

    def whole(m):
        return pl.BlockSpec(m.shape, lambda c: (0, 0))

    inner = pltpu.VMEM((wide - 2, rows, cols), F32)
    return pl.pallas_call(
        correct_kernel,
        grid=(chans,),
        in_specs=[pl.BlockSpec(memory_space=pltpu.SMEM)]
        + [whole(m) for m in (across, along, smooth_x, smooth_y, code)]
        + [spec(wide), spec(wide - 2), spec(wide - 2)]
        + [spec(depth), spec(depth), spec(HALO), spec(HALO)],
        out_specs=[spec(depth), pl.BlockSpec(memory_space=pltpu.HBM)],
        out_shape=[
            jax.ShapeDtypeStruct(own.shape, BF16),
            jax.ShapeDtypeStruct(packed, BF16),
        ],
        scratch_shapes=[
            inner,
            inner,
            pltpu.VMEM((2 * depth, rows, 2 * cols), BF16),
            pltpu.VMEM(own.shape, BF16),
            pltpu.VMEM(packed, BF16),
            pltpu.SemaphoreType.DMA((4,)),
        ],
        compiler_params=pltpu.CompilerParams(vmem_limit_bytes=60 << 20),
        cost_estimate=pl.CostEstimate(
            flops=4000000000, bytes_accessed=12000000, transcendentals=0
        ),
        name="correct",
    )(flags, across, along, smooth_x, smooth_y, code, a10, dxa, dya, own, fac, fac_lo, fac_hi)


def join_kernel(code, got, out):
    count, rows, cols = out.shape
    lines = got.shape[0]
    i = lax.broadcasted_iota(jnp.int32, (rows, lines), 0)
    one, zero = jnp.float32(1.0), jnp.float32(0.0)
    counts = None
    for h in range(2):
        place = jnp.where(i == code[h : h + 1, :], one, zero).astype(BF16)
        if h == 0:
            counts = dot(place, jnp.ones((lines, cols), BF16))
            counts = jnp.maximum(counts, 1.0)
        for n in range(count // 4):
            v = dot(place, got[:, 2 * n * cols : 2 * (n + 1) * cols])
            out[4 * n + h] = (v[:, :cols] / counts).astype(BF16)
            out[4 * n + 2 + h] = (v[:, cols:] / counts).astype(BF16)


def join(code, got, rows, cols):
    count = got.shape[1] // cols * 2
    return pl.pallas_call(
        join_kernel,
        out_shape=jax.ShapeDtypeStruct((count, rows, cols), BF16),
        compiler_params=pltpu.CompilerParams(vmem_limit_bytes=16 << 20),
        name="join",
    )(code, got)


def halo(block):
    count = lax.axis_size("gz")
    forward = [(i, i + 1) for i in range(count - 1)]
    backward = [(i + 1, i) for i in range(count - 1)]
    depth = block.shape[1]
    low = lax.ppermute(block[:, depth - HALO :], "gz", forward)
    high = lax.ppermute(block[:, :HALO], "gz", backward)
    return low, high


def swap(blocks):
    return lax.all_to_all(blocks, "tile", split_axis=0, concat_axis=0, tiled=True)


def body(images, partner, dest, offset, extent):
    ntile = lax.axis_size("tile")
    tile = lax.axis_index("tile")
    plane_idx = lax.axis_index("gz")
    nplane = lax.axis_size("gz")
    rows, chans, depth, cols = images.shape
    lines = chans * depth * rows
    own = jnp.transpose(images, (1, 2, 0, 3))
    own = lax.optimization_barrier(own)
    own_lo, own_hi = halo(own)
    spread = swap(own.reshape(ntile, lines // ntile, cols))
    picked = jnp.take(spread, partner, axis=0, mode="clip")
    fac = swap(picked).reshape(chans, depth, rows, cols)

    targets = dest[:, 0]
    order_idx = jnp.arange(ntile, dtype=jnp.int32)
    same_owner = targets[:, None] == targets[None, :]
    earlier = order_idx[:, None] > order_idx[None, :]
    slot = jnp.sum((same_owner & earlier).astype(jnp.int32), axis=1)
    slots = jnp.arange(CAP, dtype=jnp.int32)
    select = (order_idx[:, None, None] == targets[None, None, :]) & (
        slots[None, :, None] == slot[None, None, :]
    )
    label = offset * 4 + extent
    labels = jnp.sum(jnp.where(select, label[None, None, :], 0), axis=2)
    within = jnp.arange(2, dtype=jnp.int32)
    code = (targets * 8 + slot * 2)[:, None] + within[None, :]
    code = code.reshape(1, rows)
    code = jnp.concatenate([code, code + 4], axis=1)

    turn, across, along, smooth_x, smooth_y = (
        jnp.asarray(m) for m in constants(rows, cols)
    )
    smooth_x = smooth_x * (partner[tile] != tile).astype(BF16)
    flags = jnp.stack([plane_idx > 0, plane_idx < nplane - 1]).astype(F32)
    a10, dxa, dya = prepare(turn, across, along, own, own_lo, own_hi)
    fac, labels, code, a10, dxa, dya, smooth_x, flags = lax.optimization_barrier(
        (fac, labels, code, a10, dxa, dya, smooth_x, flags)
    )
    fac_lo, fac_hi = halo(fac)
    info = swap(labels)

    corrected, outgoing = correct(
        flags, across, along, smooth_x, smooth_y, code, a10, dxa, dya, own, fac, fac_lo, fac_hi, ntile
    )
    received = swap(outgoing.reshape(ntile, 8, outgoing.shape[1]))

    start, span = info // 4, info % 4
    spots = jnp.where(within < span[:, :, None], start[:, :, None] + within, -1)
    spots = spots.reshape(ntile, 2 * CAP)
    none = jnp.full_like(spots, -1)
    code_in = jnp.stack(
        [
            jnp.concatenate([spots, none], axis=1).reshape(-1),
            jnp.concatenate([none, spots], axis=1).reshape(-1),
        ]
    )
    joined = join(code_in, received.reshape(ntile * 8, -1), rows, cols)

    def home(v):
        return jnp.transpose(v.reshape(chans, depth, rows, cols), (2, 0, 1, 3))

    return home(corrected), home(joined)


def solution(mesh):
    in_specs = (P("tile", None, "gz", None), P(), P("tile", None), P("tile"), P("tile"))
    out_specs = (P("tile", None, "gz", None), P("tile", None, "gz", None))
    return jax.shard_map(body, mesh=mesh, in_specs=in_specs, out_specs=out_specs, check_vma=False)
```

```python
import math

import jax
import jax.numpy as jnp
import numpy as np
from jax import lax
from jax.experimental import pallas as pl
from jax.experimental.pallas import tpu as pltpu
from jax.sharding import PartitionSpec as P

CAP = 2
HALO = 3

gauss_raw = [math.exp(-0.5 * k * k) for k in range(-2, 3)]
gauss_taps = [w / sum(gauss_raw) for w in gauss_raw]

F32 = jnp.float32
BF16 = jnp.bfloat16


def dot(a, b):
    return jnp.dot(a, b, preferred_element_type=F32)


def split(v):
    high = v.astype(BF16)
    return high, (v - high.astype(F32)).astype(BF16)


def constants(rows, cols):
    def near(n):
        i, j = np.indices((n, n))
        return i - j

    def band(n):
        total = np.zeros((n, n), np.float32)
        for k in range(5):
            total[near(n) == k - 2] = gauss_taps[k]
        high = total.astype(BF16)
        return high, (total - high.astype(np.float32)).astype(BF16)

    turn = np.eye(cols, dtype=np.float32)[:, ::-1].astype(BF16)
    gap = near(cols)
    across = (0.5 * (gap == 1) - 0.5 * (gap == -1)).astype(BF16)
    gap = near(rows)
    along = (0.5 * (gap == -1) - 0.5 * (gap == 1)).astype(BF16)
    high, low = (m[:, ::-1] for m in band(cols))
    smooth_x = np.block([[high, low], [high, np.zeros_like(low)]])
    smooth_y = np.concatenate(band(rows), axis=0)
    return turn, across, along, smooth_x, smooth_y


def plane_of(own, own_lo, own_hi, k):
    depth = own.shape[1]
    if k < HALO:
        return own_lo, k
    if k < HALO + depth:
        return own, k - HALO
    return own_hi, k - HALO - depth


def prepare_kernel(
    turn, across, along, own, own_lo, own_hi, a10, dxa_in, dya_in, dxa_out, dya_out
):
    depth, _, cols = own.shape[1:]
    for k in range(depth + 2 * HALO):
        ref, at = plane_of(own, own_lo, own_hi, k)
        a = dot(ref[0, at], turn[...]).astype(BF16)
        a10[0, k] = a
        if 0 < k < depth + 2 * HALO - 1:
            dx, dy, n = place_of(dxa_in, dya_in, dxa_out, dya_out, depth, k)
            dx[0, n] = dot(a, across[...])
            dy[0, n] = dot(along[...], a)


def place_of(dx_in, dy_in, dx_out, dy_out, depth, k):
    if k < HALO:
        return dx_out, dy_out, k - 1
    if k < HALO + depth:
        return dx_in, dy_in, k - HALO
    return dx_out, dy_out, k - 1 - depth


def prepare(turn, across, along, own, own_lo, own_hi):
    chans, depth, rows, cols = own.shape
    wide = depth + 2 * HALO
    edge = 2 * (HALO - 1)

    def spec(n):
        return pl.BlockSpec((1, n, rows, cols), lambda c: (c, 0, 0, 0))

    def whole(m):
        return pl.BlockSpec(m.shape, lambda c: (0, 0))

    def shape(n, dtype):
        return jax.ShapeDtypeStruct((chans, n, rows, cols), dtype)

    return pl.pallas_call(
        prepare_kernel,
        grid=(chans,),
        in_specs=[whole(turn), whole(across), whole(along)]
        + [spec(depth), spec(HALO), spec(HALO)],
        out_specs=[spec(wide), spec(depth), spec(depth), spec(edge), spec(edge)],
        out_shape=[shape(wide, BF16)]
        + [shape(depth, F32)] * 2
        + [shape(edge, F32)] * 2,
        compiler_params=pltpu.CompilerParams(vmem_limit_bytes=60 << 20),
        name="prepare",
    )(turn, across, along, own, own_lo, own_hi)


def inner_kernel(across, along, a10, dxa, dya, fac, part, dxb, dyb):
    depth, rows, cols = fac.shape[1:]
    half = jnp.float32(0.5)
    for z in range(depth):
        now = fac[0, z]
        dxb[z] = dot(now, across[...])
        if z % 2 == 1:
            dy = dot(along[...], jnp.concatenate([fac[0, z - 1], now], axis=1))
            dyb[z - 1] = dy[:, :cols]
            dyb[z] = dy[:, cols:]

    step = 64

    def chunk(r, carry):
        at_rows = pl.ds(pl.multiple_of(r * step, step), step)
        a = [a10[0, HALO + z, at_rows, :].astype(F32) for z in range(depth)]
        b = [fac[0, z, at_rows, :].astype(F32) for z in range(depth)]
        for z in range(depth):
            ya, yb = dya[0, z, at_rows, :], dyb[z, at_rows, :]
            xa, xb = dxa[0, z, at_rows, :], dxb[z, at_rows, :]
            p1 = a[z] * b[z] + ya * yb + xa * xb
            p2 = b[z] * b[z] + yb * yb + xb * xb
            if 0 < z < depth - 1:
                dza = (a[z + 1] - a[z - 1]) * half
                dzb = (b[z + 1] - b[z - 1]) * half
                p1, p2 = p1 + dza * dzb, p2 + dzb * dzb
            part[0, 2 * z, at_rows, :] = p1
            part[0, 2 * z + 1, at_rows, :] = p2
        return carry

    lax.fori_loop(0, rows // step, chunk, 0)


def inner(across, along, a10, dxa, dya, fac):
    chans, depth, rows, cols = fac.shape

    def spec(n):
        return pl.BlockSpec((1, n, rows, cols), lambda c: (c, 0, 0, 0))

    def whole(m):
        return pl.BlockSpec(m.shape, lambda c: (0, 0))

    held = pltpu.VMEM((depth, rows, cols), F32)
    return pl.pallas_call(
        inner_kernel,
        grid=(chans,),
        in_specs=[whole(across), whole(along)]
        + [spec(depth + 2 * HALO), spec(depth), spec(depth), spec(depth)],
        out_specs=spec(2 * depth),
        out_shape=jax.ShapeDtypeStruct((chans, 2 * depth, rows, cols), F32),
        scratch_shapes=[held, held],
        compiler_params=pltpu.CompilerParams(vmem_limit_bytes=60 << 20),
        cost_estimate=pl.CostEstimate(
            flops=1000000000, bytes_accessed=10000000, transcendentals=0
        ),
        name="inner",
    )(across, along, a10, dxa, dya, fac)


def pack(code, planes, out, held, sems):
    chans, _, rows, cols = planes.shape
    step = held.shape[0] // sems.shape[0]
    copies = []
    for m in range(sems.shape[0]):
        at = pl.ds(m * step, step)
        i = lax.broadcasted_iota(jnp.int32, (step, 2 * rows), 0) + m * step
        pick = jnp.where(i == code[...], jnp.float32(1.0), jnp.float32(0.0)).astype(BF16)
        for n in range(chans):
            left = planes[n, 0:2].reshape(2 * rows, cols)
            right = planes[n, 2:4].reshape(2 * rows, cols)
            v = dot(pick, jnp.concatenate([left, right], axis=1))
            held[m * step : (m + 1) * step, 2 * n * cols : 2 * (n + 1) * cols] = v.astype(BF16)
        copies.append(pltpu.make_async_copy(held.at[at], out.at[at], sems.at[m]))
        copies[-1].start()
    for copy in copies:
        copy.wait()


def correct_kernel(
    flags,
    across,
    along,
    smooth_x,
    smooth_y,
    code,
    a10,
    dxa,
    dya,
    part,
    own,
    fac,
    fac_lo,
    fac_hi,
    out,
    sent,
    dxb,
    dyb,
    deep,
    kept,
    held,
    sems,
):
    chan = pl.program_id(0)
    depth, rows, cols = fac.shape[1:]
    wide = depth + 2 * HALO
    low, high = flags[0], flags[1]
    half = jnp.float32(0.5)
    for k in (1, 2, wide - 3, wide - 2):
        ref, at = plane_of(fac, fac_lo, fac_hi, k)
        now = ref[0, at]
        n = k - 1 if k < HALO else k - 1 - depth
        dxb[n] = dot(now, across[...])
        if n % 2 == 1:
            dy = dot(along[...], jnp.concatenate([before, now], axis=1))
            dyb[n - 1] = dy[:, :cols]
            dyb[n] = dy[:, cols:]
        before = now

    step = 32

    def chunk(r, carry):
        at_rows = pl.ds(pl.multiple_of(r * step, step), step)

        def a_of(k):
            return a10[0, k, at_rows, :].astype(F32)

        def b_of(k):
            ref, at = plane_of(fac, fac_lo, fac_hi, k)
            return ref[0, at, at_rows, :].astype(F32)

        one = [None] * depth
        two = [None] * depth
        for k in range(1, wide - 1):
            z = k - HALO
            if 0 <= z < depth:
                p1, p2 = part[0, 2 * z, at_rows, :], part[0, 2 * z + 1, at_rows, :]
            if not 0 < z < depth - 1:
                dza = (a_of(k + 1) - a_of(k - 1)) * half
                dzb = (b_of(k + 1) - b_of(k - 1)) * half
                if 0 <= z < depth:
                    p1, p2 = p1 + dza * dzb, p2 + dzb * dzb
                else:
                    n = k - 1 if k < HALO else k - 1 - depth
                    av, bv = a_of(k), b_of(k)
                    ya, yb = dya[0, n, at_rows, :], dyb[n, at_rows, :]
                    xa, xb = dxa[0, n, at_rows, :], dxb[n, at_rows, :]
                    p1 = av * bv + ya * yb + dza * dzb + xa * xb
                    p2 = bv * bv + yb * yb + dzb * dzb + xb * xb
            if k < HALO:
                p1, p2 = p1 * low, p2 * low
            if k >= HALO + depth:
                p1, p2 = p1 * high, p2 * high
            for t in range(3):
                v1, v2 = gauss_taps[t] * p1, gauss_taps[t] * p2
                for z in {k - HALO + 2 - t, k - HALO - 2 + t}:
                    if 0 <= z < depth:
                        one[z] = v1 if one[z] is None else one[z] + v1
                        two[z] = v2 if two[z] is None else two[z] + v2
        for z in range(depth):
            for s, v in ((0, one[z]), (1, two[z])):
                h, l = split(v)
                deep[2 * z + s, at_rows, :cols] = h
                deep[2 * z + s, at_rows, cols:] = l
        return carry

    lax.fori_loop(0, rows // step, chunk, 0)

    for z in range(depth):
        parts = []
        for s in range(2):
            r = dot(deep[2 * z + s], smooth_x[...])
            parts.append(split(r[:, :cols] + r[:, cols:]))
        r_hi = jnp.concatenate([parts[0][0], parts[1][0]], axis=1)
        r_lo = jnp.concatenate([parts[0][1], parts[1][1]], axis=1)
        main = dot(smooth_y[...], r_hi)
        q = main[:rows] + main[rows:] + dot(smooth_y[:rows], r_lo)
        a = own[0, z].astype(F32)
        done = (a * (q[:, :cols] + 1.0) / (q[:, cols:] + 1.0)).astype(BF16)
        out[0, z] = done
        kept[chan, z] = done

    @pl.when(chan == kept.shape[0] - 1)
    def _():
        pack(code, kept, sent, held, sems)


def correct(
    flags, across, along, smooth_x, smooth_y, code, a10, dxa, dya, part, own, fac, fac_lo, fac_hi, blocks
):
    chans, depth, rows, cols = own.shape
    wide = depth + 2 * HALO
    packed = (blocks * 8, chans * depth // 2 * cols)

    def spec(n):
        return pl.BlockSpec((1, n, rows, cols), lambda c: (c, 0, 0, 0))

    def whole(m):
        return pl.BlockSpec(m.shape, lambda c: (0, 0))

    edge = 2 * (HALO - 1)
    held = pltpu.VMEM((edge, rows, cols), F32)
    return pl.pallas_call(
        correct_kernel,
        grid=(chans,),
        in_specs=[pl.BlockSpec(memory_space=pltpu.SMEM)]
        + [whole(m) for m in (across, along, smooth_x, smooth_y, code)]
        + [spec(wide), spec(edge), spec(edge), spec(2 * depth)]
        + [spec(depth), spec(depth), spec(HALO), spec(HALO)],
        out_specs=[spec(depth), pl.BlockSpec(memory_space=pltpu.HBM)],
        out_shape=[
            jax.ShapeDtypeStruct(own.shape, BF16),
            jax.ShapeDtypeStruct(packed, BF16),
        ],
        scratch_shapes=[
            held,
            held,
            pltpu.VMEM((2 * depth, rows, 2 * cols), BF16),
            pltpu.VMEM(own.shape, BF16),
            pltpu.VMEM(packed, BF16),
            pltpu.SemaphoreType.DMA((4,)),
        ],
        compiler_params=pltpu.CompilerParams(vmem_limit_bytes=60 << 20),
        cost_estimate=pl.CostEstimate(
            flops=4000000000, bytes_accessed=12000000, transcendentals=0
        ),
        name="correct",
    )(flags, across, along, smooth_x, smooth_y, code, a10, dxa, dya, part, own, fac, fac_lo, fac_hi)


def join_kernel(code, got, out):
    count, rows, cols = out.shape
    lines = got.shape[0]
    i = lax.broadcasted_iota(jnp.int32, (rows, lines), 0)
    one, zero = jnp.float32(1.0), jnp.float32(0.0)
    counts = None
    for h in range(2):
        place = jnp.where(i == code[h : h + 1, :], one, zero).astype(BF16)
        if h == 0:
            counts = dot(place, jnp.ones((lines, cols), BF16))
            counts = jnp.maximum(counts, 1.0)
        for n in range(count // 4):
            v = dot(place, got[:, 2 * n * cols : 2 * (n + 1) * cols])
            out[4 * n + h] = (v[:, :cols] / counts).astype(BF16)
            out[4 * n + 2 + h] = (v[:, cols:] / counts).astype(BF16)


def join(code, got, rows, cols):
    count = got.shape[1] // cols * 2
    return pl.pallas_call(
        join_kernel,
        out_shape=jax.ShapeDtypeStruct((count, rows, cols), BF16),
        compiler_params=pltpu.CompilerParams(vmem_limit_bytes=16 << 20),
        name="join",
    )(code, got)


def halo(block):
    count = lax.axis_size("gz")
    forward = [(i, i + 1) for i in range(count - 1)]
    backward = [(i + 1, i) for i in range(count - 1)]
    depth = block.shape[1]
    low = lax.ppermute(block[:, depth - HALO :], "gz", forward)
    high = lax.ppermute(block[:, :HALO], "gz", backward)
    return low, high


def swap(blocks):
    return lax.all_to_all(blocks, "tile", split_axis=0, concat_axis=0, tiled=True)


def body(images, partner, dest, offset, extent):
    ntile = lax.axis_size("tile")
    tile = lax.axis_index("tile")
    plane_idx = lax.axis_index("gz")
    nplane = lax.axis_size("gz")
    rows, chans, depth, cols = images.shape
    lines = chans * depth * rows
    own = jnp.transpose(images, (1, 2, 0, 3))
    own = lax.optimization_barrier(own)
    own_lo, own_hi = halo(own)
    spread = swap(own.reshape(ntile, lines // ntile, cols))
    picked = jnp.take(spread, partner, axis=0, mode="clip")
    fac = swap(picked).reshape(chans, depth, rows, cols)

    targets = dest[:, 0]
    order_idx = jnp.arange(ntile, dtype=jnp.int32)
    same_owner = targets[:, None] == targets[None, :]
    earlier = order_idx[:, None] > order_idx[None, :]
    slot = jnp.sum((same_owner & earlier).astype(jnp.int32), axis=1)
    slots = jnp.arange(CAP, dtype=jnp.int32)
    select = (order_idx[:, None, None] == targets[None, None, :]) & (
        slots[None, :, None] == slot[None, None, :]
    )
    label = offset * 4 + extent
    labels = jnp.sum(jnp.where(select, label[None, None, :], 0), axis=2)
    within = jnp.arange(2, dtype=jnp.int32)
    code = (targets * 8 + slot * 2)[:, None] + within[None, :]
    code = code.reshape(1, rows)
    code = jnp.concatenate([code, code + 4], axis=1)

    turn, across, along, smooth_x, smooth_y = (
        jnp.asarray(m) for m in constants(rows, cols)
    )
    smooth_x = smooth_x * (partner[tile] != tile).astype(BF16)
    flags = jnp.stack([plane_idx > 0, plane_idx < nplane - 1]).astype(F32)
    a10, dxa_in, dya_in, dxa, dya = prepare(turn, across, along, own, own_lo, own_hi)
    fac, labels, code, a10, dxa_in, dya_in, dxa, dya, smooth_x, flags = lax.optimization_barrier(
        (fac, labels, code, a10, dxa_in, dya_in, dxa, dya, smooth_x, flags)
    )
    fac_lo, fac_hi = halo(fac)
    info = swap(labels)

    part = inner(across, along, a10, dxa_in, dya_in, fac)
    corrected, outgoing = correct(
        flags,
        across,
        along,
        smooth_x,
        smooth_y,
        code,
        a10,
        dxa,
        dya,
        part,
        own,
        fac,
        fac_lo,
        fac_hi,
        ntile,
    )
    received = swap(outgoing.reshape(ntile, 8, outgoing.shape[1]))

    start, span = info // 4, info % 4
    spots = jnp.where(within < span[:, :, None], start[:, :, None] + within, -1)
    spots = spots.reshape(ntile, 2 * CAP)
    none = jnp.full_like(spots, -1)
    code_in = jnp.stack(
        [
            jnp.concatenate([spots, none], axis=1).reshape(-1),
            jnp.concatenate([none, spots], axis=1).reshape(-1),
        ]
    )
    joined = join(code_in, received.reshape(ntile * 8, -1), rows, cols)

    def home(v):
        return jnp.transpose(v.reshape(chans, depth, rows, cols), (2, 0, 1, 3))

    return home(corrected), home(joined)


def solution(mesh):
    in_specs = (P("tile", None, "gz", None), P(), P("tile", None), P("tile"), P("tile"))
    out_specs = (P("tile", None, "gz", None), P("tile", None, "gz", None))
    return jax.shard_map(body, mesh=mesh, in_specs=in_specs, out_specs=out_specs, check_vma=False)
```

```python
import math

import jax
import jax.numpy as jnp
import numpy as np
from jax import lax
from jax.experimental import pallas as pl
from jax.experimental.pallas import tpu as pltpu
from jax.sharding import PartitionSpec as P

CAP = 2
HALO = 3

gauss_raw = [math.exp(-0.5 * k * k) for k in range(-2, 3)]
gauss_taps = [w / sum(gauss_raw) for w in gauss_raw]

F32 = jnp.float32
BF16 = jnp.bfloat16


def dot(a, b):
    return jnp.dot(a, b, preferred_element_type=F32)


def split(v):
    high = v.astype(BF16)
    return high, (v - high.astype(F32)).astype(BF16)


def constants(rows, cols):
    def near(n):
        i, j = np.indices((n, n))
        return i - j

    def band(n):
        total = np.zeros((n, n), np.float32)
        for k in range(5):
            total[near(n) == k - 2] = gauss_taps[k]
        high = total.astype(BF16)
        return high, (total - high.astype(np.float32)).astype(BF16)

    turn = np.eye(cols, dtype=np.float32)[:, ::-1].astype(BF16)
    gap = near(cols)
    across = (0.5 * (gap == 1) - 0.5 * (gap == -1)).astype(BF16)
    gap = near(rows)
    along = (0.5 * (gap == -1) - 0.5 * (gap == 1)).astype(BF16)
    high, low = (m[:, ::-1] for m in band(cols))
    smooth_x = np.block([[high, low], [high, np.zeros_like(low)]])
    smooth_y = np.concatenate(band(rows), axis=0)
    return turn, across, along, smooth_x, smooth_y


def plane_of(own, own_lo, own_hi, k):
    depth = own.shape[1]
    if k < HALO:
        return own_lo, k
    if k < HALO + depth:
        return own, k - HALO
    return own_hi, k - HALO - depth


def prepare_kernel(turn, own, own_lo, own_hi, a_in, a_out):
    depth = own.shape[1]
    for k in range(depth + 2 * HALO):
        ref, at = plane_of(own, own_lo, own_hi, k)
        a = dot(ref[0, at], turn[...]).astype(BF16)
        if HALO <= k < HALO + depth:
            a_in[0, k - HALO] = a
        else:
            a_out[0, k if k < HALO else k - depth] = a


def prepare(turn, own, own_lo, own_hi):
    chans, depth, rows, cols = own.shape

    def spec(n):
        return pl.BlockSpec((1, n, rows, cols), lambda c: (c, 0, 0, 0))

    def shape(n):
        return jax.ShapeDtypeStruct((chans, n, rows, cols), BF16)

    return pl.pallas_call(
        prepare_kernel,
        grid=(chans,),
        in_specs=[pl.BlockSpec(turn.shape, lambda c: (0, 0))]
        + [spec(depth), spec(HALO), spec(HALO)],
        out_specs=[spec(depth), spec(2 * HALO)],
        out_shape=[shape(depth), shape(2 * HALO)],
        compiler_params=pltpu.CompilerParams(vmem_limit_bytes=60 << 20),
        name="prepare",
    )(turn, own, own_lo, own_hi)


def differences(a, f, across, along, n, dxa, dxb, dya, dyb):
    cols = a.shape[1]
    dxa[n] = dot(a, across[...])
    dxb[n] = dot(f, across[...])
    dy = dot(along[...], jnp.concatenate([a, f], axis=1))
    dya[n] = dy[:, :cols]
    dyb[n] = dy[:, cols:]


def inner_kernel(across, along, own, fac, part, dxa, dxb, dya, dyb):
    depth, rows, _ = fac.shape[1:]
    half = jnp.float32(0.5)
    for z in range(depth):
        differences(own[0, z], fac[0, z], across, along, z, dxa, dxb, dya, dyb)

    step = 64

    def chunk(r, carry):
        at_rows = pl.ds(pl.multiple_of(r * step, step), step)
        a = [own[0, z, at_rows, :].astype(F32) for z in range(depth)]
        b = [fac[0, z, at_rows, :].astype(F32) for z in range(depth)]
        for z in range(depth):
            ya, yb = dya[z, at_rows, :], dyb[z, at_rows, :]
            xa, xb = dxa[z, at_rows, :], dxb[z, at_rows, :]
            p1 = a[z] * b[z] + ya * yb + xa * xb
            p2 = b[z] * b[z] + yb * yb + xb * xb
            if 0 < z < depth - 1:
                dza = (a[z + 1] - a[z - 1]) * half
                dzb = (b[z + 1] - b[z - 1]) * half
                p1, p2 = p1 + dza * dzb, p2 + dzb * dzb
            part[0, 2 * z, at_rows, :] = p1
            part[0, 2 * z + 1, at_rows, :] = p2
        return carry

    lax.fori_loop(0, rows // step, chunk, 0)


def inner(across, along, own, fac):
    chans, depth, rows, cols = fac.shape

    def spec(n):
        return pl.BlockSpec((1, n, rows, cols), lambda c: (c, 0, 0, 0))

    def whole(m):
        return pl.BlockSpec(m.shape, lambda c: (0, 0))

    return pl.pallas_call(
        inner_kernel,
        grid=(chans,),
        in_specs=[whole(across), whole(along), spec(depth), spec(depth)],
        out_specs=spec(2 * depth),
        out_shape=jax.ShapeDtypeStruct((chans, 2 * depth, rows, cols), F32),
        scratch_shapes=[pltpu.VMEM((depth, rows, cols), F32)] * 4,
        compiler_params=pltpu.CompilerParams(vmem_limit_bytes=60 << 20),
        cost_estimate=pl.CostEstimate(
            flops=1000000000, bytes_accessed=10000000, transcendentals=0
        ),
        name="inner",
    )(across, along, own, fac)


def pack(code, planes, out, held, sems):
    chans, _, rows, cols = planes.shape
    step = held.shape[0] // sems.shape[0]
    copies = []
    for m in range(sems.shape[0]):
        at = pl.ds(m * step, step)
        i = lax.broadcasted_iota(jnp.int32, (step, 2 * rows), 0) + m * step
        pick = jnp.where(i == code[...], jnp.float32(1.0), jnp.float32(0.0)).astype(BF16)
        for n in range(chans):
            left = planes[n, 0:2].reshape(2 * rows, cols)
            right = planes[n, 2:4].reshape(2 * rows, cols)
            v = dot(pick, jnp.concatenate([left, right], axis=1))
            held[m * step : (m + 1) * step, 2 * n * cols : 2 * (n + 1) * cols] = v.astype(BF16)
        copies.append(pltpu.make_async_copy(held.at[at], out.at[at], sems.at[m]))
        copies[-1].start()
    for copy in copies:
        copy.wait()


def correct_kernel(
    flags,
    across,
    along,
    smooth_x,
    smooth_y,
    code,
    a_in,
    a_out,
    part,
    own,
    fac,
    fac_lo,
    fac_hi,
    out,
    sent,
    dxa,
    dxb,
    dya,
    dyb,
    deep,
    kept,
    held,
    sems,
):
    chan = pl.program_id(0)
    depth, rows, cols = fac.shape[1:]
    wide = depth + 2 * HALO
    low, high = flags[0], flags[1]
    half = jnp.float32(0.5)
    def a_at(k):
        if k < HALO:
            return a_out, k
        if k < HALO + depth:
            return a_in, k - HALO
        return a_out, k - depth

    for k in (1, 2, wide - 3, wide - 2):
        own_ref, own_at = a_at(k)
        ref, at = plane_of(fac, fac_lo, fac_hi, k)
        n = k - 1 if k < HALO else k - 1 - depth
        differences(own_ref[0, own_at], ref[0, at], across, along, n, dxa, dxb, dya, dyb)

    step = 32

    def chunk(r, carry):
        at_rows = pl.ds(pl.multiple_of(r * step, step), step)

        def a_of(k):
            ref, at = a_at(k)
            return ref[0, at, at_rows, :].astype(F32)

        def b_of(k):
            ref, at = plane_of(fac, fac_lo, fac_hi, k)
            return ref[0, at, at_rows, :].astype(F32)

        one = [None] * depth
        two = [None] * depth
        for k in range(1, wide - 1):
            z = k - HALO
            if 0 <= z < depth:
                p1, p2 = part[0, 2 * z, at_rows, :], part[0, 2 * z + 1, at_rows, :]
            if not 0 < z < depth - 1:
                dza = (a_of(k + 1) - a_of(k - 1)) * half
                dzb = (b_of(k + 1) - b_of(k - 1)) * half
                if 0 <= z < depth:
                    p1, p2 = p1 + dza * dzb, p2 + dzb * dzb
                else:
                    n = k - 1 if k < HALO else k - 1 - depth
                    av, bv = a_of(k), b_of(k)
                    ya, yb = dya[n, at_rows, :], dyb[n, at_rows, :]
                    xa, xb = dxa[n, at_rows, :], dxb[n, at_rows, :]
                    p1 = av * bv + ya * yb + dza * dzb + xa * xb
                    p2 = bv * bv + yb * yb + dzb * dzb + xb * xb
            if k < HALO:
                p1, p2 = p1 * low, p2 * low
            if k >= HALO + depth:
                p1, p2 = p1 * high, p2 * high
            for t in range(3):
                v1, v2 = gauss_taps[t] * p1, gauss_taps[t] * p2
                for z in {k - HALO + 2 - t, k - HALO - 2 + t}:
                    if 0 <= z < depth:
                        one[z] = v1 if one[z] is None else one[z] + v1
                        two[z] = v2 if two[z] is None else two[z] + v2
        for z in range(depth):
            for s, v in ((0, one[z]), (1, two[z])):
                h, l = split(v)
                deep[2 * z + s, at_rows, :cols] = h
                deep[2 * z + s, at_rows, cols:] = l
        return carry

    lax.fori_loop(0, rows // step, chunk, 0)

    for z in range(depth):
        parts = []
        for s in range(2):
            r = dot(deep[2 * z + s], smooth_x[...])
            parts.append(split(r[:, :cols] + r[:, cols:]))
        r_hi = jnp.concatenate([parts[0][0], parts[1][0]], axis=1)
        r_lo = jnp.concatenate([parts[0][1], parts[1][1]], axis=1)
        main = dot(smooth_y[...], r_hi)
        q = main[:rows] + main[rows:] + dot(smooth_y[:rows], r_lo)
        a = own[0, z].astype(F32)
        done = (a * (q[:, :cols] + 1.0) / (q[:, cols:] + 1.0)).astype(BF16)
        out[0, z] = done
        kept[chan, z] = done

    @pl.when(chan == kept.shape[0] - 1)
    def _():
        pack(code, kept, sent, held, sems)


def correct(
    flags, across, along, smooth_x, smooth_y, code, a_in, a_out, part, own, fac, fac_lo, fac_hi, blocks
):
    chans, depth, rows, cols = own.shape
    packed = (blocks * 8, chans * depth // 2 * cols)

    def spec(n):
        return pl.BlockSpec((1, n, rows, cols), lambda c: (c, 0, 0, 0))

    def whole(m):
        return pl.BlockSpec(m.shape, lambda c: (0, 0))

    edge = 2 * (HALO - 1)
    held = pltpu.VMEM((edge, rows, cols), F32)
    return pl.pallas_call(
        correct_kernel,
        grid=(chans,),
        in_specs=[pl.BlockSpec(memory_space=pltpu.SMEM)]
        + [whole(m) for m in (across, along, smooth_x, smooth_y, code)]
        + [spec(depth), spec(2 * HALO), spec(2 * depth)]
        + [spec(depth), spec(depth), spec(HALO), spec(HALO)],
        out_specs=[spec(depth), pl.BlockSpec(memory_space=pltpu.HBM)],
        out_shape=[
            jax.ShapeDtypeStruct(own.shape, BF16),
            jax.ShapeDtypeStruct(packed, BF16),
        ],
        scratch_shapes=[
            held,
            held,
            held,
            held,
            pltpu.VMEM((2 * depth, rows, 2 * cols), BF16),
            pltpu.VMEM(own.shape, BF16),
            pltpu.VMEM(packed, BF16),
            pltpu.SemaphoreType.DMA((4,)),
        ],
        compiler_params=pltpu.CompilerParams(vmem_limit_bytes=60 << 20),
        cost_estimate=pl.CostEstimate(
            flops=4000000000, bytes_accessed=12000000, transcendentals=0
        ),
        name="correct",
    )(flags, across, along, smooth_x, smooth_y, code, a_in, a_out, part, own, fac, fac_lo, fac_hi)


def join_kernel(code, got, out):
    count, rows, cols = out.shape
    lines = got.shape[0]
    i = lax.broadcasted_iota(jnp.int32, (rows, lines), 0)
    one, zero = jnp.float32(1.0), jnp.float32(0.0)
    counts = None
    for h in range(2):
        place = jnp.where(i == code[h : h + 1, :], one, zero).astype(BF16)
        if h == 0:
            counts = dot(place, jnp.ones((lines, cols), BF16))
            counts = jnp.maximum(counts, 1.0)
        for n in range(count // 4):
            v = dot(place, got[:, 2 * n * cols : 2 * (n + 1) * cols])
            out[4 * n + h] = (v[:, :cols] / counts).astype(BF16)
            out[4 * n + 2 + h] = (v[:, cols:] / counts).astype(BF16)


def join(code, got, rows, cols):
    count = got.shape[1] // cols * 2
    return pl.pallas_call(
        join_kernel,
        out_shape=jax.ShapeDtypeStruct((count, rows, cols), BF16),
        compiler_params=pltpu.CompilerParams(vmem_limit_bytes=16 << 20),
        name="join",
    )(code, got)


def halo(block):
    count = lax.axis_size("gz")
    forward = [(i, i + 1) for i in range(count - 1)]
    backward = [(i + 1, i) for i in range(count - 1)]
    depth = block.shape[1]
    low = lax.ppermute(block[:, depth - HALO :], "gz", forward)
    high = lax.ppermute(block[:, :HALO], "gz", backward)
    return low, high


def swap(blocks):
    return lax.all_to_all(blocks, "tile", split_axis=0, concat_axis=0, tiled=True)


def body(images, partner, dest, offset, extent):
    ntile = lax.axis_size("tile")
    tile = lax.axis_index("tile")
    plane_idx = lax.axis_index("gz")
    nplane = lax.axis_size("gz")
    rows, chans, depth, cols = images.shape
    lines = chans * depth * rows
    own = jnp.transpose(images, (1, 2, 0, 3))
    own = lax.optimization_barrier(own)
    own_lo, own_hi = halo(own)
    spread = swap(own.reshape(ntile, lines // ntile, cols))
    picked = jnp.take(spread, partner, axis=0, mode="clip")
    fac = swap(picked).reshape(chans, depth, rows, cols)

    targets = dest[:, 0]
    order_idx = jnp.arange(ntile, dtype=jnp.int32)
    same_owner = targets[:, None] == targets[None, :]
    earlier = order_idx[:, None] > order_idx[None, :]
    slot = jnp.sum((same_owner & earlier).astype(jnp.int32), axis=1)
    slots = jnp.arange(CAP, dtype=jnp.int32)
    select = (order_idx[:, None, None] == targets[None, None, :]) & (
        slots[None, :, None] == slot[None, None, :]
    )
    label = offset * 4 + extent
    labels = jnp.sum(jnp.where(select, label[None, None, :], 0), axis=2)
    within = jnp.arange(2, dtype=jnp.int32)
    code = (targets * 8 + slot * 2)[:, None] + within[None, :]
    code = code.reshape(1, rows)
    code = jnp.concatenate([code, code + 4], axis=1)

    turn, across, along, smooth_x, smooth_y = (
        jnp.asarray(m) for m in constants(rows, cols)
    )
    smooth_x = smooth_x * (partner[tile] != tile).astype(BF16)
    flags = jnp.stack([plane_idx > 0, plane_idx < nplane - 1]).astype(F32)
    a_in, a_out = prepare(turn, own, own_lo, own_hi)
    fac, labels, code, a_in, a_out, smooth_x, flags = lax.optimization_barrier(
        (fac, labels, code, a_in, a_out, smooth_x, flags)
    )
    fac_lo, fac_hi = halo(fac)
    info = swap(labels)

    part = inner(across, along, a_in, fac)
    corrected, outgoing = correct(
        flags,
        across,
        along,
        smooth_x,
        smooth_y,
        code,
        a_in,
        a_out,
        part,
        own,
        fac,
        fac_lo,
        fac_hi,
        ntile,
    )
    received = swap(outgoing.reshape(ntile, 8, outgoing.shape[1]))

    start, span = info // 4, info % 4
    spots = jnp.where(within < span[:, :, None], start[:, :, None] + within, -1)
    spots = spots.reshape(ntile, 2 * CAP)
    none = jnp.full_like(spots, -1)
    code_in = jnp.stack(
        [
            jnp.concatenate([spots, none], axis=1).reshape(-1),
            jnp.concatenate([none, spots], axis=1).reshape(-1),
        ]
    )
    joined = join(code_in, received.reshape(ntile * 8, -1), rows, cols)

    def home(v):
        return jnp.transpose(v.reshape(chans, depth, rows, cols), (2, 0, 1, 3))

    return home(corrected), home(joined)


def solution(mesh):
    in_specs = (P("tile", None, "gz", None), P(), P("tile", None), P("tile"), P("tile"))
    out_specs = (P("tile", None, "gz", None), P("tile", None, "gz", None))
    return jax.shard_map(body, mesh=mesh, in_specs=in_specs, out_specs=out_specs, check_vma=False)
```

```python
import math

import jax
import jax.numpy as jnp
import numpy as np
from jax import lax
from jax.experimental import pallas as pl
from jax.experimental.pallas import tpu as pltpu
from jax.sharding import PartitionSpec as P

CAP = 2
HALO = 3

gauss_raw = [math.exp(-0.5 * k * k) for k in range(-2, 3)]
gauss_taps = [w / sum(gauss_raw) for w in gauss_raw]

F32 = jnp.float32
BF16 = jnp.bfloat16


def dot(a, b):
    return jnp.dot(a, b, preferred_element_type=F32)


def split(v):
    high = v.astype(BF16)
    return high, (v - high.astype(F32)).astype(BF16)


def constants(rows, cols):
    def near(n):
        i, j = np.indices((n, n))
        return i - j

    def band(n):
        total = np.zeros((n, n), np.float32)
        for k in range(5):
            total[near(n) == k - 2] = gauss_taps[k]
        high = total.astype(BF16)
        return high, (total - high.astype(np.float32)).astype(BF16)

    turn = np.eye(cols, dtype=np.float32)[:, ::-1].astype(BF16)
    gap = near(cols)
    across = (0.5 * (gap == 1) - 0.5 * (gap == -1)).astype(BF16)
    gap = near(rows)
    along = (0.5 * (gap == -1) - 0.5 * (gap == 1)).astype(BF16)
    high, low = (m[:, ::-1] for m in band(cols))
    smooth_x = np.block([[high, low], [high, np.zeros_like(low)]])
    smooth_y = np.concatenate(band(rows), axis=0)
    return turn, across, along, smooth_x, smooth_y


def plane_of(own, own_lo, own_hi, k):
    depth = own.shape[1]
    if k < HALO:
        return own_lo, k
    if k < HALO + depth:
        return own, k - HALO
    return own_hi, k - HALO - depth


def prepare_kernel(turn, own, own_lo, own_hi, a10):
    depth = own.shape[1]
    for k in range(depth + 2 * HALO):
        ref, at = plane_of(own, own_lo, own_hi, k)
        a10[0, k] = dot(ref[0, at], turn[...]).astype(BF16)


def prepare(turn, own, own_lo, own_hi):
    chans, depth, rows, cols = own.shape
    wide = depth + 2 * HALO

    def spec(n):
        return pl.BlockSpec((1, n, rows, cols), lambda c: (c, 0, 0, 0))

    return pl.pallas_call(
        prepare_kernel,
        grid=(chans,),
        in_specs=[pl.BlockSpec(turn.shape, lambda c: (0, 0))]
        + [spec(depth), spec(HALO), spec(HALO)],
        out_specs=spec(wide),
        out_shape=jax.ShapeDtypeStruct((chans, wide, rows, cols), BF16),
        compiler_params=pltpu.CompilerParams(vmem_limit_bytes=60 << 20),
        name="prepare",
    )(turn, own, own_lo, own_hi)


def pack(code, planes, out, held, sems):
    chans, _, rows, cols = planes.shape
    step = held.shape[0] // sems.shape[0]
    copies = []
    for m in range(sems.shape[0]):
        at = pl.ds(m * step, step)
        i = lax.broadcasted_iota(jnp.int32, (step, 2 * rows), 0) + m * step
        pick = jnp.where(i == code[...], jnp.float32(1.0), jnp.float32(0.0)).astype(BF16)
        for n in range(chans):
            left = planes[n, 0:2].reshape(2 * rows, cols)
            right = planes[n, 2:4].reshape(2 * rows, cols)
            v = dot(pick, jnp.concatenate([left, right], axis=1))
            held[m * step : (m + 1) * step, 2 * n * cols : 2 * (n + 1) * cols] = v.astype(BF16)
        copies.append(pltpu.make_async_copy(held.at[at], out.at[at], sems.at[m]))
        copies[-1].start()
    for copy in copies:
        copy.wait()


def correct_kernel(
    flags,
    across,
    along,
    smooth_x,
    smooth_y,
    code,
    a10,
    own,
    fac,
    fac_lo,
    fac_hi,
    out,
    sent,
    dxa,
    dxb,
    dya,
    dyb,
    deep,
    kept,
    held,
    sems,
):
    chan = pl.program_id(0)
    depth, rows, cols = fac.shape[1:]
    wide = depth + 2 * HALO
    low, high = flags[0], flags[1]
    half = jnp.float32(0.5)
    for k in range(1, wide - 1):
        ref, at = plane_of(fac, fac_lo, fac_hi, k)
        a, f = a10[0, k], ref[0, at]
        dxa[k - 1] = dot(a, across[...])
        dxb[k - 1] = dot(f, across[...])
        dy = dot(along[...], jnp.concatenate([a, f], axis=1))
        dya[k - 1] = dy[:, :cols]
        dyb[k - 1] = dy[:, cols:]

    step = 32

    def chunk(r, carry):
        at_rows = pl.ds(pl.multiple_of(r * step, step), step)

        def a_of(k):
            return a10[0, k, at_rows, :].astype(F32)

        def b_of(k):
            ref, at = plane_of(fac, fac_lo, fac_hi, k)
            return ref[0, at, at_rows, :].astype(F32)

        one = [None] * depth
        two = [None] * depth
        a_last, av, a_next = None, a_of(0), a_of(1)
        b_last, bv, b_next = None, b_of(0), b_of(1)
        for k in range(1, wide - 1):
            a_last, av, a_next = av, a_next, a_of(k + 1)
            b_last, bv, b_next = bv, b_next, b_of(k + 1)
            dza = (a_next - a_last) * half
            dzb = (b_next - b_last) * half
            ya, yb = dya[k - 1, at_rows, :], dyb[k - 1, at_rows, :]
            xa, xb = dxa[k - 1, at_rows, :], dxb[k - 1, at_rows, :]
            p1 = av * bv + ya * yb + dza * dzb + xa * xb
            p2 = bv * bv + yb * yb + dzb * dzb + xb * xb
            if k < HALO:
                p1, p2 = p1 * low, p2 * low
            if k >= HALO + depth:
                p1, p2 = p1 * high, p2 * high
            for t in range(3):
                v1, v2 = gauss_taps[t] * p1, gauss_taps[t] * p2
                for z in {k - HALO + 2 - t, k - HALO - 2 + t}:
                    if 0 <= z < depth:
                        one[z] = v1 if one[z] is None else one[z] + v1
                        two[z] = v2 if two[z] is None else two[z] + v2
        for z in range(depth):
            for s, v in ((0, one[z]), (1, two[z])):
                h, l = split(v)
                deep[2 * z + s, at_rows, :cols] = h
                deep[2 * z + s, at_rows, cols:] = l
        return carry

    lax.fori_loop(0, rows // step, chunk, 0)

    for z in range(depth):
        parts = []
        for s in range(2):
            r = dot(deep[2 * z + s], smooth_x[...])
            parts.append(split(r[:, :cols] + r[:, cols:]))
        r_hi = jnp.concatenate([parts[0][0], parts[1][0]], axis=1)
        r_lo = jnp.concatenate([parts[0][1], parts[1][1]], axis=1)
        main = dot(smooth_y[...], r_hi)
        q = main[:rows] + main[rows:] + dot(smooth_y[:rows], r_lo)
        a = own[0, z].astype(F32)
        done = (a * (q[:, :cols] + 1.0) / (q[:, cols:] + 1.0)).astype(BF16)
        out[0, z] = done
        kept[chan, z] = done

    @pl.when(chan == kept.shape[0] - 1)
    def _():
        pack(code, kept, sent, held, sems)


def correct(
    flags, across, along, smooth_x, smooth_y, code, a10, own, fac, fac_lo, fac_hi, blocks
):
    chans, depth, rows, cols = own.shape
    wide = depth + 2 * HALO
    packed = (blocks * 8, chans * depth // 2 * cols)

    def spec(n):
        return pl.BlockSpec((1, n, rows, cols), lambda c: (c, 0, 0, 0))

    def whole(m):
        return pl.BlockSpec(m.shape, lambda c: (0, 0))

    inner = pltpu.VMEM((wide - 2, rows, cols), F32)
    return pl.pallas_call(
        correct_kernel,
        grid=(chans,),
        in_specs=[pl.BlockSpec(memory_space=pltpu.SMEM)]
        + [whole(m) for m in (across, along, smooth_x, smooth_y, code)]
        + [spec(wide)]
        + [spec(depth), spec(depth), spec(HALO), spec(HALO)],
        out_specs=[spec(depth), pl.BlockSpec(memory_space=pltpu.HBM)],
        out_shape=[
            jax.ShapeDtypeStruct(own.shape, BF16),
            jax.ShapeDtypeStruct(packed, BF16),
        ],
        scratch_shapes=[
            inner,
            inner,
            inner,
            inner,
            pltpu.VMEM((2 * depth, rows, 2 * cols), BF16),
            pltpu.VMEM(own.shape, BF16),
            pltpu.VMEM(packed, BF16),
            pltpu.SemaphoreType.DMA((4,)),
        ],
        compiler_params=pltpu.CompilerParams(vmem_limit_bytes=60 << 20),
        cost_estimate=pl.CostEstimate(
            flops=4000000000, bytes_accessed=12000000, transcendentals=0
        ),
        name="correct",
    )(flags, across, along, smooth_x, smooth_y, code, a10, own, fac, fac_lo, fac_hi)


def join_kernel(code, got, out):
    count, rows, cols = out.shape
    lines = got.shape[0]
    i = lax.broadcasted_iota(jnp.int32, (rows, lines), 0)
    one, zero = jnp.float32(1.0), jnp.float32(0.0)
    counts = None
    for h in range(2):
        place = jnp.where(i == code[h : h + 1, :], one, zero).astype(BF16)
        if h == 0:
            counts = dot(place, jnp.ones((lines, cols), BF16))
            counts = jnp.maximum(counts, 1.0)
        for n in range(count // 4):
            v = dot(place, got[:, 2 * n * cols : 2 * (n + 1) * cols])
            out[4 * n + h] = (v[:, :cols] / counts).astype(BF16)
            out[4 * n + 2 + h] = (v[:, cols:] / counts).astype(BF16)


def join(code, got, rows, cols):
    count = got.shape[1] // cols * 2
    return pl.pallas_call(
        join_kernel,
        out_shape=jax.ShapeDtypeStruct((count, rows, cols), BF16),
        compiler_params=pltpu.CompilerParams(vmem_limit_bytes=16 << 20),
        name="join",
    )(code, got)


def halo(block):
    count = lax.axis_size("gz")
    forward = [(i, i + 1) for i in range(count - 1)]
    backward = [(i + 1, i) for i in range(count - 1)]
    depth = block.shape[1]
    low = lax.ppermute(block[:, depth - HALO :], "gz", forward)
    high = lax.ppermute(block[:, :HALO], "gz", backward)
    return low, high


def swap(blocks):
    return lax.all_to_all(blocks, "tile", split_axis=0, concat_axis=0, tiled=True)


def body(images, partner, dest, offset, extent):
    ntile = lax.axis_size("tile")
    tile = lax.axis_index("tile")
    plane_idx = lax.axis_index("gz")
    nplane = lax.axis_size("gz")
    rows, chans, depth, cols = images.shape
    lines = chans * depth * rows
    own = jnp.transpose(images, (1, 2, 0, 3))
    own = lax.optimization_barrier(own)
    own_lo, own_hi = halo(own)
    spread = swap(own.reshape(ntile, lines // ntile, cols))
    picked = jnp.take(spread, partner, axis=0, mode="clip")
    fac = swap(picked).reshape(chans, depth, rows, cols)

    targets = dest[:, 0]
    order_idx = jnp.arange(ntile, dtype=jnp.int32)
    same_owner = targets[:, None] == targets[None, :]
    earlier = order_idx[:, None] > order_idx[None, :]
    slot = jnp.sum((same_owner & earlier).astype(jnp.int32), axis=1)
    slots = jnp.arange(CAP, dtype=jnp.int32)
    select = (order_idx[:, None, None] == targets[None, None, :]) & (
        slots[None, :, None] == slot[None, None, :]
    )
    label = offset * 4 + extent
    labels = jnp.sum(jnp.where(select, label[None, None, :], 0), axis=2)
    within = jnp.arange(2, dtype=jnp.int32)
    code = (targets * 8 + slot * 2)[:, None] + within[None, :]
    code = code.reshape(1, rows)
    code = jnp.concatenate([code, code + 4], axis=1)

    turn, across, along, smooth_x, smooth_y = (
        jnp.asarray(m) for m in constants(rows, cols)
    )
    smooth_x = smooth_x * (partner[tile] != tile).astype(BF16)
    flags = jnp.stack([plane_idx > 0, plane_idx < nplane - 1]).astype(F32)
    a10 = prepare(turn, own, own_lo, own_hi)
    fac, labels, code, a10, smooth_x, flags = lax.optimization_barrier(
        (fac, labels, code, a10, smooth_x, flags)
    )
    fac_lo, fac_hi = halo(fac)
    info = swap(labels)

    corrected, outgoing = correct(
        flags, across, along, smooth_x, smooth_y, code, a10, own, fac, fac_lo, fac_hi, ntile
    )
    received = swap(outgoing.reshape(ntile, 8, outgoing.shape[1]))

    start, span = info // 4, info % 4
    spots = jnp.where(within < span[:, :, None], start[:, :, None] + within, -1)
    spots = spots.reshape(ntile, 2 * CAP)
    none = jnp.full_like(spots, -1)
    code_in = jnp.stack(
        [
            jnp.concatenate([spots, none], axis=1).reshape(-1),
            jnp.concatenate([none, spots], axis=1).reshape(-1),
        ]
    )
    joined = join(code_in, received.reshape(ntile * 8, -1), rows, cols)

    def home(v):
        return jnp.transpose(v.reshape(chans, depth, rows, cols), (2, 0, 1, 3))

    return home(corrected), home(joined)


def solution(mesh):
    in_specs = (P("tile", None, "gz", None), P(), P("tile", None), P("tile"), P("tile"))
    out_specs = (P("tile", None, "gz", None), P("tile", None, "gz", None))
    return jax.shard_map(body, mesh=mesh, in_specs=in_specs, out_specs=out_specs, check_vma=False)
```

```python
import math

import jax
import jax.numpy as jnp
import numpy as np
from jax import lax
from jax.experimental import pallas as pl
from jax.experimental.pallas import tpu as pltpu
from jax.sharding import PartitionSpec as P

CAP = 2
HALO = 3

gauss_raw = [math.exp(-0.5 * k * k) for k in range(-2, 3)]
gauss_taps = [w / sum(gauss_raw) for w in gauss_raw]

F32 = jnp.float32
BF16 = jnp.bfloat16


def dot(a, b):
    return jnp.dot(a, b, preferred_element_type=F32)


def split(v):
    high = v.astype(BF16)
    return high, (v - high.astype(F32)).astype(BF16)


def constants(rows, cols):
    def near(n):
        i, j = np.indices((n, n))
        return i - j

    def band(n):
        total = np.zeros((n, n), np.float32)
        for k in range(5):
            total[near(n) == k - 2] = gauss_taps[k]
        high = total.astype(BF16)
        return high, (total - high.astype(np.float32)).astype(BF16)

    turn = np.eye(cols, dtype=np.float32)[:, ::-1].astype(BF16)
    gap = near(cols)
    across = (0.5 * (gap == 1) - 0.5 * (gap == -1)).astype(BF16)
    gap = near(rows)
    along = (0.5 * (gap == -1) - 0.5 * (gap == 1)).astype(BF16)
    high, low = (m[:, ::-1] for m in band(cols))
    smooth_x = np.block([[high, low], [high, np.zeros_like(low)]])
    smooth_y = np.concatenate(band(rows), axis=0)
    return turn, across, along, smooth_x, smooth_y


def plane_of(own, own_lo, own_hi, k):
    depth = own.shape[1]
    if k < HALO:
        return own_lo, k
    if k < HALO + depth:
        return own, k - HALO
    return own_hi, k - HALO - depth


def prepare_kernel(turn, across, along, own, own_lo, own_hi, a10, dxa, dya):
    depth, _, cols = own.shape[1:]
    for k in range(depth + 2 * HALO):
        ref, at = plane_of(own, own_lo, own_hi, k)
        a = dot(ref[0, at], turn[...]).astype(BF16)
        a10[0, k] = a
        if 0 < k < depth + 2 * HALO - 1:
            dxa[0, k - 1] = dot(a, across[...])
            if k % 2 == 0:
                dy = dot(along[...], jnp.concatenate([before, a], axis=1))
                dya[0, k - 2] = dy[:, :cols]
                dya[0, k - 1] = dy[:, cols:]
        before = a


def prepare(turn, across, along, own, own_lo, own_hi):
    chans, depth, rows, cols = own.shape
    wide = depth + 2 * HALO

    def spec(n):
        return pl.BlockSpec((1, n, rows, cols), lambda c: (c, 0, 0, 0))

    def whole(m):
        return pl.BlockSpec(m.shape, lambda c: (0, 0))

    def shape(n, dtype):
        return jax.ShapeDtypeStruct((chans, n, rows, cols), dtype)

    return pl.pallas_call(
        prepare_kernel,
        grid=(chans,),
        in_specs=[whole(turn), whole(across), whole(along)]
        + [spec(depth), spec(HALO), spec(HALO)],
        out_specs=[spec(wide), spec(wide - 2), spec(wide - 2)],
        out_shape=[shape(wide, BF16), shape(wide - 2, F32), shape(wide - 2, F32)],
        compiler_params=pltpu.CompilerParams(vmem_limit_bytes=60 << 20),
        name="prepare",
    )(turn, across, along, own, own_lo, own_hi)


def pack(code, planes, out, held, sems):
    chans, _, rows, cols = planes.shape
    step = held.shape[0] // sems.shape[0]
    copies = []
    for m in range(sems.shape[0]):
        at = pl.ds(m * step, step)
        i = lax.broadcasted_iota(jnp.int32, (step, 2 * rows), 0) + m * step
        pick = jnp.where(i == code[...], jnp.float32(1.0), jnp.float32(0.0)).astype(BF16)
        for n in range(chans):
            left = planes[n, 0:2].reshape(2 * rows, cols)
            right = planes[n, 2:4].reshape(2 * rows, cols)
            v = dot(pick, jnp.concatenate([left, right], axis=1))
            held[m * step : (m + 1) * step, 2 * n * cols : 2 * (n + 1) * cols] = v.astype(BF16)
        copies.append(pltpu.make_async_copy(held.at[at], out.at[at], sems.at[m]))
        copies[-1].start()
    for copy in copies:
        copy.wait()


def correct_kernel(
    flags,
    across,
    along,
    smooth_x,
    smooth_y,
    code,
    a10,
    dxa,
    dya,
    own,
    fac,
    fac_lo,
    fac_hi,
    out,
    sent,
    dxb,
    dyb,
    deep,
    kept,
    held,
    sems,
):
    chan = pl.program_id(0)
    depth, rows, cols = fac.shape[1:]
    wide = depth + 2 * HALO
    low, high = flags[0], flags[1]
    half = jnp.float32(0.5)
    for k in range(1, wide - 1):
        ref, at = plane_of(fac, fac_lo, fac_hi, k)
        now = ref[0, at]
        dxb[k - 1] = dot(now, across[...])
        if k % 2 == 0:
            dy = dot(along[...], jnp.concatenate([before, now], axis=1))
            dyb[k - 2] = dy[:, :cols]
            dyb[k - 1] = dy[:, cols:]
        before = now

    step = 16

    def chunk(r, carry):
        at_rows = pl.ds(pl.multiple_of(r * step, step), step)

        def a_of(k):
            return a10[0, k, at_rows, :].astype(F32)

        def b_of(k):
            ref, at = plane_of(fac, fac_lo, fac_hi, k)
            return ref[0, at, at_rows, :].astype(F32)

        one = [None] * depth
        two = [None] * depth
        a_last, av, a_next = None, a_of(0), a_of(1)
        b_last, bv, b_next = None, b_of(0), b_of(1)
        for k in range(1, wide - 1):
            a_last, av, a_next = av, a_next, a_of(k + 1)
            b_last, bv, b_next = bv, b_next, b_of(k + 1)
            dza = (a_next - a_last) * half
            dzb = (b_next - b_last) * half
            ya, yb = dya[0, k - 1, at_rows, :], dyb[k - 1, at_rows, :]
            xa, xb = dxa[0, k - 1, at_rows, :], dxb[k - 1, at_rows, :]
            p1 = av * bv + ya * yb + dza * dzb + xa * xb
            p2 = bv * bv + yb * yb + dzb * dzb + xb * xb
            if k < HALO:
                p1, p2 = p1 * low, p2 * low
            if k >= HALO + depth:
                p1, p2 = p1 * high, p2 * high
            for t in range(3):
                v1, v2 = gauss_taps[t] * p1, gauss_taps[t] * p2
                for z in {k - HALO + 2 - t, k - HALO - 2 + t}:
                    if 0 <= z < depth:
                        one[z] = v1 if one[z] is None else one[z] + v1
                        two[z] = v2 if two[z] is None else two[z] + v2
        for z in range(depth):
            for s, v in ((0, one[z]), (1, two[z])):
                h, l = split(v)
                deep[2 * z + s, at_rows, :cols] = h
                deep[2 * z + s, at_rows, cols:] = l
        return carry

    lax.fori_loop(0, rows // step, chunk, 0)

    for z in range(depth):
        parts = []
        for s in range(2):
            r = dot(deep[2 * z + s], smooth_x[...])
            parts.append(split(r[:, :cols] + r[:, cols:]))
        r_hi = jnp.concatenate([parts[0][0], parts[1][0]], axis=1)
        r_lo = jnp.concatenate([parts[0][1], parts[1][1]], axis=1)
        main = dot(smooth_y[...], r_hi)
        q = main[:rows] + main[rows:] + dot(smooth_y[:rows], r_lo)
        a = own[0, z].astype(F32)
        done = (a * (q[:, :cols] + 1.0) / (q[:, cols:] + 1.0)).astype(BF16)
        out[0, z] = done
        kept[chan, z] = done

    @pl.when(chan == kept.shape[0] - 1)
    def _():
        pack(code, kept, sent, held, sems)


def correct(
    flags, across, along, smooth_x, smooth_y, code, a10, dxa, dya, own, fac, fac_lo, fac_hi, blocks
):
    chans, depth, rows, cols = own.shape
    wide = depth + 2 * HALO
    packed = (blocks * 8, chans * depth // 2 * cols)

    def spec(n):
        return pl.BlockSpec((1, n, rows, cols), lambda c: (c, 0, 0, 0))

    def whole(m):
        return pl.BlockSpec(m.shape, lambda c: (0, 0))

    inner = pltpu.VMEM((wide - 2, rows, cols), F32)
    return pl.pallas_call(
        correct_kernel,
        grid=(chans,),
        in_specs=[pl.BlockSpec(memory_space=pltpu.SMEM)]
        + [whole(m) for m in (across, along, smooth_x, smooth_y, code)]
        + [spec(wide), spec(wide - 2), spec(wide - 2)]
        + [spec(depth), spec(depth), spec(HALO), spec(HALO)],
        out_specs=[spec(depth), pl.BlockSpec(memory_space=pltpu.HBM)],
        out_shape=[
            jax.ShapeDtypeStruct(own.shape, BF16),
            jax.ShapeDtypeStruct(packed, BF16),
        ],
        scratch_shapes=[
            inner,
            inner,
            pltpu.VMEM((2 * depth, rows, 2 * cols), BF16),
            pltpu.VMEM(own.shape, BF16),
            pltpu.VMEM(packed, BF16),
            pltpu.SemaphoreType.DMA((4,)),
        ],
        compiler_params=pltpu.CompilerParams(vmem_limit_bytes=60 << 20),
        cost_estimate=pl.CostEstimate(
            flops=4000000000, bytes_accessed=12000000, transcendentals=0
        ),
        name="correct",
    )(flags, across, along, smooth_x, smooth_y, code, a10, dxa, dya, own, fac, fac_lo, fac_hi)


def join_kernel(code, got, out):
    count, rows, cols = out.shape
    lines = got.shape[0]
    i = lax.broadcasted_iota(jnp.int32, (rows, lines), 0)
    one, zero = jnp.float32(1.0), jnp.float32(0.0)
    counts = None
    for h in range(2):
        place = jnp.where(i == code[h : h + 1, :], one, zero).astype(BF16)
        if h == 0:
            counts = dot(place, jnp.ones((lines, cols), BF16))
            counts = jnp.maximum(counts, 1.0)
        for n in range(count // 4):
            v = dot(place, got[:, 2 * n * cols : 2 * (n + 1) * cols])
            out[4 * n + h] = (v[:, :cols] / counts).astype(BF16)
            out[4 * n + 2 + h] = (v[:, cols:] / counts).astype(BF16)


def join(code, got, rows, cols):
    count = got.shape[1] // cols * 2
    return pl.pallas_call(
        join_kernel,
        out_shape=jax.ShapeDtypeStruct((count, rows, cols), BF16),
        compiler_params=pltpu.CompilerParams(vmem_limit_bytes=16 << 20),
        name="join",
    )(code, got)


def halo(block):
    count = lax.axis_size("gz")
    forward = [(i, i + 1) for i in range(count - 1)]
    backward = [(i + 1, i) for i in range(count - 1)]
    depth = block.shape[1]
    low = lax.ppermute(block[:, depth - HALO :], "gz", forward)
    high = lax.ppermute(block[:, :HALO], "gz", backward)
    return low, high


def swap(blocks):
    return lax.all_to_all(blocks, "tile", split_axis=0, concat_axis=0, tiled=True)


def body(images, partner, dest, offset, extent):
    ntile = lax.axis_size("tile")
    tile = lax.axis_index("tile")
    plane_idx = lax.axis_index("gz")
    nplane = lax.axis_size("gz")
    rows, chans, depth, cols = images.shape
    lines = chans * depth * rows
    own = jnp.transpose(images, (1, 2, 0, 3))
    own = lax.optimization_barrier(own)
    own_lo, own_hi = halo(own)
    spread = swap(own.reshape(ntile, lines // ntile, cols))
    picked = jnp.take(spread, partner, axis=0, mode="clip")
    fac = swap(picked).reshape(chans, depth, rows, cols)

    targets = dest[:, 0]
    order_idx = jnp.arange(ntile, dtype=jnp.int32)
    same_owner = targets[:, None] == targets[None, :]
    earlier = order_idx[:, None] > order_idx[None, :]
    slot = jnp.sum((same_owner & earlier).astype(jnp.int32), axis=1)
    slots = jnp.arange(CAP, dtype=jnp.int32)
    select = (order_idx[:, None, None] == targets[None, None, :]) & (
        slots[None, :, None] == slot[None, None, :]
    )
    label = offset * 4 + extent
    labels = jnp.sum(jnp.where(select, label[None, None, :], 0), axis=2)
    within = jnp.arange(2, dtype=jnp.int32)
    code = (targets * 8 + slot * 2)[:, None] + within[None, :]
    code = code.reshape(1, rows)
    code = jnp.concatenate([code, code + 4], axis=1)

    turn, across, along, smooth_x, smooth_y = (
        jnp.asarray(m) for m in constants(rows, cols)
    )
    smooth_x = smooth_x * (partner[tile] != tile).astype(BF16)
    flags = jnp.stack([plane_idx > 0, plane_idx < nplane - 1]).astype(F32)
    a10, dxa, dya = prepare(turn, across, along, own, own_lo, own_hi)
    fac, labels, code, a10, dxa, dya, smooth_x, flags = lax.optimization_barrier(
        (fac, labels, code, a10, dxa, dya, smooth_x, flags)
    )
    fac_lo, fac_hi = halo(fac)
    info = swap(labels)

    corrected, outgoing = correct(
        flags, across, along, smooth_x, smooth_y, code, a10, dxa, dya, own, fac, fac_lo, fac_hi, ntile
    )
    received = swap(outgoing.reshape(ntile, 8, outgoing.shape[1]))

    start, span = info // 4, info % 4
    spots = jnp.where(within < span[:, :, None], start[:, :, None] + within, -1)
    spots = spots.reshape(ntile, 2 * CAP)
    none = jnp.full_like(spots, -1)
    code_in = jnp.stack(
        [
            jnp.concatenate([spots, none], axis=1).reshape(-1),
            jnp.concatenate([none, spots], axis=1).reshape(-1),
        ]
    )
    joined = join(code_in, received.reshape(ntile * 8, -1), rows, cols)

    def home(v):
        return jnp.transpose(v.reshape(chans, depth, rows, cols), (2, 0, 1, 3))

    return home(corrected), home(joined)


def solution(mesh):
    in_specs = (P("tile", None, "gz", None), P(), P("tile", None), P("tile"), P("tile"))
    out_specs = (P("tile", None, "gz", None), P("tile", None, "gz", None))
    return jax.shard_map(body, mesh=mesh, in_specs=in_specs, out_specs=out_specs, check_vma=False)
```
